256 devices in a mesh: dom: 64 (over y, z_lo, x, core), rep: 4 (over z_hi).
Axes of the slice: x: 4, y: 4, z: 8 (z_hi: 4, z_lo: 2; z = z_hi * 2 + z_lo), core: 2. Of those that a mesh axis runs over, the one named last changes fastest.
Arguments:
- entities: float32 [16384, 512], P('dom'), may hold values from -1.5 to 1.5
- ent_accum: float32 [16384], P('dom'), may hold values from 0.5 to 20
- relations: float32 [8, 512, 512], P('rep'), may hold values from -0.25 to 0.25
- rel_accum: float32 [8, 512, 512], P('rep'), may hold values from 29.4912 to 294.912
- heads: int32 [3, 196608], P(None, ('dom', 'rep')), may hold values from 0 to 255
- tails: int32 [3, 196608], P(None, ('dom', 'rep')), may hold values from 0 to 255
- relation_ids: int32 [3, 196608], P(None, ('dom', 'rep')), may hold values from 0 to 1
- negatives: int32 [3, 65536], P(None, ('dom', 'rep')), may hold values from 0 to 255
Outputs:
- new_entities: float32 [16384, 512], P('dom')
- new_ent_accum: float32 [16384], P('dom')
- new_relations: float32 [8, 512, 512], P('rep')
- new_rel_accum: float32 [8, 512, 512], P('rep')
The draws below stay inside these ranges and needn't reach their ends.
Inputs may be any that keep to these rules, and one draw needn't show every extreme that they name: `negatives`: rows within the named partition; some rows are named far more often than others.
All inputs are finite; a program needn't handle non-finite values.
Results may differ from the reference program's by a relative error of at most 0.0077.
Values may be sent and summed in bfloat16 or wider, within the bound.
No kernel may reach another device: no remote copies, remote signals or barrier semaphores. Data moves between devices by JAX's collectives and lax.ppermute only.
A program may use at most 64 MiB of HBM per device.

```python
import math
import jax
import jax.numpy as jnp
import numpy as np
from jax import lax

D = 512
ENT_DEV = 256
E_DEV = 768
NCAP = 4
REL_DEV = 2
ROUNDS = 3
ENTITIES = 16384
NEG_DEV = 256
REL = 8
N_DOM = 64
N_REP = 4
DEVICES = 256


def set_ends(result, rng, smallest, top_value):
    longest = result.shape.index(max(result.shape))
    spots = []
    for shift in (0, 1):
        where = [jax.random.randint(jax.random.fold_in(rng, axis), (), 0, length) for axis, length in enumerate(result.shape)]
        where[longest] = (where[longest] + shift) % result.shape[longest]
        spots.append(tuple(where))
    return result.at[spots[0]].set(smallest).at[spots[1]].set(top_value)


def levels(own_key, dims, split, smallest, largest):
    def one(position, blocks):
        steps = jax.random.uniform(jax.random.fold_in(jax.random.fold_in(own_key, 6), position), (blocks,), jnp.float32, smallest / len(split), largest / len(split))
        return jnp.repeat(jnp.exp(steps), dims[position] // blocks).reshape((-1,) + (1,) * (len(dims) - position - 1))

    gain = one(*split[0])
    for cut in split[1:]:
        gain = gain * one(*cut)
    return gain


def rank_bounds(number_of, lean):
    loads = [(1 << 20) // math.isqrt(grade ** lean) + 1 for grade in range(1, number_of + 1)]
    spread = 1 + sum(loads) // (1 << 30)
    return np.cumsum(np.array([max(1, weight // spread) for weight in loads]))


def ranked(key, extent, amount, skew):
    listing = rank_bounds(amount, skew)
    ticket = jax.random.randint(jax.random.fold_in(key, 1), extent, 0, int(listing[amount - 1]))
    standing = jnp.searchsorted(jnp.asarray(listing, jnp.int32), ticket, side="right")
    return jax.random.permutation(jax.random.fold_in(key, 2), amount)[standing].astype(jnp.int32)


def noise(key, shape, deviation, reach, cuts=(), kind=jnp.bfloat16):
    entries = jax.random.normal(key, shape, jnp.float32) * deviation
    if len(cuts) > 0:
        entries = levels(key, shape, cuts, -0.22, 0.18) * entries
    return jnp.clip(entries, min=-reach, max=reach).astype(kind)


def setup_inputs(seed: int = 0) -> dict:
    seeds = jax.random.split(jax.random.key(seed), 9)
    entities = noise(seeds[0], (ENTITIES, D), 0.25, 1.5, ((0, 64),), jnp.float32)
    ent_accum = jnp.clip(jnp.exp(math.log(20.0) - 3.6888795 * jax.random.uniform(seeds[1], (ENTITIES,), jnp.float32) ** levels(seeds[1], (ENTITIES,), ((0, 64),), -0.2, 0.2)), 0.5, 20.0)
    relations = noise(seeds[2], (REL, D, D), (22.0 / D), 0.25, ((0, 4),), jnp.float32)
    rel_accum = jnp.clip(jnp.exp(math.log(294.912) - 2.3025851 * jax.random.uniform(seeds[3], (REL, D, D), jnp.float32) ** levels(seeds[3], (REL, D, D), ((0, 4),), -0.2, 0.2)), 29.4912, 294.912)
    heads = set_ends(jax.random.randint(seeds[4], (ROUNDS, DEVICES * E_DEV), 0, ENT_DEV), jax.random.fold_in(seeds[4], 1), 0, ENT_DEV - 1).astype(jnp.int32)
    tails = set_ends(jax.random.randint(seeds[5], (ROUNDS, DEVICES * E_DEV), 0, ENT_DEV), jax.random.fold_in(seeds[5], 1), 0, ENT_DEV - 1).astype(jnp.int32)
    relation_ids = set_ends(jax.random.randint(seeds[6], (ROUNDS, DEVICES * E_DEV), 0, REL_DEV), jax.random.fold_in(seeds[6], 1), 0, REL_DEV - 1).astype(jnp.int32)
    negatives = set_ends(ranked(seeds[7], (ROUNDS, DEVICES * NEG_DEV), ENT_DEV, 2), jax.random.fold_in(seeds[7], 3), 0, ENT_DEV - 1).astype(jnp.int32)
    return dict(entities=entities, ent_accum=ent_accum, relations=relations, rel_accum=rel_accum, heads=heads, tails=tails, relation_ids=relation_ids, negatives=negatives)


negative_weight = 0.0625
entity_rate = 0.05
relation_rate = 0.02

def bucket_terms(head_rows, tail_rows, neg_rows, rel_cat, rel_back, rel_ids):
    edges = head_rows.shape[0]
    width = head_rows.shape[1]
    kinds = rel_cat.shape[1] // width
    picks = (rel_ids[:, None] == jnp.arange(kinds, dtype=jnp.int32)[None, :]).astype(jnp.float32)
    proj = jnp.dot(head_rows, rel_cat, preferred_element_type=jnp.float32).reshape(edges, kinds, width)
    query = lax.optimization_barrier(jnp.sum(proj * picks[:, :, None], axis=1)).astype(jnp.bfloat16)
    columns = jnp.concatenate([tail_rows, neg_rows], axis=0)
    scores = lax.dot_general(query, columns, (((1,), (1,)), ((), ())), preferred_element_type=jnp.float32)
    diagonal = jnp.arange(edges, dtype=jnp.int32)[:, None] == jnp.arange(columns.shape[0], dtype=jnp.int32)[None, :]
    probs = jax.nn.sigmoid(scores)
    dscore = jnp.where(diagonal, probs - 1.0, negative_weight * probs).astype(jnp.bfloat16)
    dquery = jnp.dot(dscore, columns, preferred_element_type=jnp.float32).astype(jnp.bfloat16)
    dcolumns = lax.dot_general(dscore, query, (((0,), (0,)), ((), ())), preferred_element_type=jnp.float32)
    dhead_all = jnp.dot(dquery, rel_back, preferred_element_type=jnp.float32).reshape(edges, kinds, width)
    dhead = lax.optimization_barrier(jnp.sum(dhead_all * picks[:, :, None], axis=1))
    masked = (head_rows[:, None, :] * picks[:, :, None].astype(head_rows.dtype)).reshape(edges, kinds * width)
    drel = lax.dot_general(masked, dquery, (((0,), (0,)), ((), ())), preferred_element_type=jnp.float32)
    return (dhead, dcolumns[:edges], dcolumns[edges:], drel.reshape(kinds, width, width))

def reference(entities, ent_accum, relations, rel_accum, heads, tails, relation_ids, negatives):
    parts = N_DOM
    groups = N_REP
    rows = ENT_DEV
    width = D
    rel_bf = relations.astype(jnp.bfloat16).reshape(groups, REL_DEV, width, width)
    cats = rel_bf.transpose(0, 2, 1, 3).reshape(groups, width, REL_DEV * width)
    backs = rel_bf.transpose(0, 3, 1, 2).reshape(groups, width, REL_DEV * width)
    rel_total = jnp.zeros((groups, REL_DEV, width, width), jnp.float32)
    owners = jnp.arange(NEG_DEV, dtype=jnp.int32) // NCAP
    for rnd in range(ROUNDS):
        offset = rnd + 1
        ent_bf = entities.astype(jnp.bfloat16)
        head_all = heads[rnd].reshape(parts * groups, E_DEV)
        tail_all = tails[rnd].reshape(parts * groups, E_DEV)
        kind_all = relation_ids[rnd].reshape(parts * groups, E_DEV)
        neg_all = negatives[rnd].reshape(parts * groups, NEG_DEV)

        def visit(carry, device):
            grads, rgrad = carry
            part = device // groups
            group = device % groups
            partner = (part + offset) % parts
            hidx = lax.dynamic_index_in_dim(head_all, device, 0, keepdims=False)
            tidx = lax.dynamic_index_in_dim(tail_all, device, 0, keepdims=False)
            kidx = lax.dynamic_index_in_dim(kind_all, device, 0, keepdims=False)
            nidx = lax.dynamic_index_in_dim(neg_all, device, 0, keepdims=False)
            hglob = (part * rows + hidx).astype(jnp.int32)
            tglob = (partner * rows + tidx).astype(jnp.int32)
            nglob = (owners * rows + nidx).astype(jnp.int32)
            rel_cat = lax.dynamic_index_in_dim(cats, group, 0, keepdims=False)
            rel_back = lax.dynamic_index_in_dim(backs, group, 0, keepdims=False)
            dhead, dtail, dneg, drel = bucket_terms(jnp.take(ent_bf, hglob, axis=0), jnp.take(ent_bf, tglob, axis=0), jnp.take(ent_bf, nglob, axis=0), rel_cat, rel_back, kidx)
            grads = grads.at[jnp.concatenate([hglob, tglob, nglob])].add(jnp.concatenate([dhead, dtail, dneg], axis=0))
            rgrad = rgrad.at[group].add(drel)
            return ((grads, rgrad), None)
        start = (jnp.zeros((parts * rows, width), jnp.float32), rel_total)
        (grads, rel_total), _ = lax.scan(visit, start, jnp.arange(parts * groups, dtype=jnp.int32))
        ent_accum = ent_accum + lax.optimization_barrier(jnp.mean(grads * grads, axis=-1))
        entities = entities - entity_rate * grads / jnp.sqrt(ent_accum)[:, None]
    total = rel_total.reshape(groups * REL_DEV, width, width)
    new_rel_accum = rel_accum + total * total
    new_relations = relations - relation_rate * total / jnp.sqrt(new_rel_accum)
    return (entities, ent_accum, new_relations, new_rel_accum)
```

```python
import jax
import jax.numpy as jnp
from jax import lax
from jax.experimental import pallas as pl
from jax.experimental.pallas import tpu as pltpu
from jax.sharding import PartitionSpec as P

NCAP = 4
ROUNDS = 3
LANES = 128

negative_weight = 0.0625
entity_rate = 0.05
relation_rate = 0.02

BF = jnp.bfloat16
F32 = jnp.float32


def call(kernel, outs, *args, flops=0, aliases=None, vmem=24):
    outs = [jax.ShapeDtypeStruct(s, d) for s, d in outs]
    moved = sum(a.size * a.dtype.itemsize for a in args)
    moved += sum(o.size * o.dtype.itemsize for o in outs)
    return pl.pallas_call(
        kernel,
        out_shape=outs,
        in_specs=[pl.BlockSpec(memory_space=pltpu.VMEM)] * len(args),
        out_specs=[pl.BlockSpec(memory_space=pltpu.VMEM)] * len(outs),
        input_output_aliases=aliases or {},
        compiler_params=pltpu.CompilerParams(vmem_limit_bytes=vmem << 20),
        cost_estimate=pl.CostEstimate(flops=flops, bytes_accessed=moved, transcendentals=0),
    )(*args)


def nn(a, b):
    return jnp.dot(a, b, preferred_element_type=F32)


def nt(a, b):
    return lax.dot_general(a, b, (((1,), (1,)), ((), ())), preferred_element_type=F32)


def tn(a, b):
    return lax.dot_general(a, b, (((0,), (0,)), ((), ())), preferred_element_type=F32)


def iota(shape, dim):
    return lax.broadcasted_iota(jnp.int32, shape, dim)


def one_hot_rows(count, index):
    return (iota((count, index.shape[1]), 0) == index).astype(F32).astype(BF)


def all_ways(block, axes):
    return lax.all_to_all(block, axes, split_axis=0, concat_axis=0, tiled=True)


def from_behind(block, axis, distance):
    n = lax.axis_size(axis)
    return lax.ppermute(block, axis, [((i - distance) % n, i) for i in range(n)])


def fill_container(out_ref, ent_bf, idx_x):
    width = ent_bf.shape[1]
    cuts = width // LANES
    picked = tn(one_hot_rows(ent_bf.shape[0], idx_x), ent_bf)
    which = (iota((idx_x.shape[1], LANES), 0) // NCAP) % cuts
    out = picked[:, :LANES]
    for cs in range(1, cuts):
        out = jnp.where(which == cs, picked[:, cs * LANES : (cs + 1) * LANES], out)
    out_ref[...] = out.astype(BF)


def serve_kernel(ent_ref, idx_ref, out_ref):
    fill_container(out_ref, ent_ref[...], idx_ref[...])


def tail_kernel(ent_ref, rel_ref, par_ref, head_ref, tail_ref, kind_ref, tq_ref, at_ref, n_ref, dtail_ref):
    rows = ent_ref.shape[0]
    kinds = rel_ref.shape[0]
    ent = ent_ref[...]
    for t in range(kinds):
        tq_ref[t * rows : (t + 1) * rows, :] = nn(ent, rel_ref[t]).astype(BF)
    pick_q = one_hot_rows(kinds * rows, kind_ref[...] * rows + head_ref[...])
    pick_t = one_hot_rows(rows, tail_ref[...])
    ones = jnp.ones((LANES, pick_q.shape[1]), F32).astype(BF)
    joint = nt(pick_q, pick_t)
    n = nt(pick_q, ones)
    c = nt(ones, pick_t)[:1]
    n_ref[...] = n
    tq = tq_ref[...]
    par = par_ref[...]
    prob = jax.nn.sigmoid(nt(tq, par))
    weight = (negative_weight * n[:, :1]) * c
    at = (weight * prob + joint * ((1.0 - negative_weight) * prob - 1.0)).astype(BF)
    at_ref[...] = at
    dtail_ref[...] = tn(at, tq).astype(BF)


def neg_kernel(con_ref, tq_ref, n_ref, neg_ref, an_ref, dneg_ref):
    slots, width = neg_ref.shape
    cuts = width // LANES
    con = con_ref[...]
    slot = iota((slots, con.shape[0]), 0)
    row = iota((slots, con.shape[0]), 1) - ((slot // NCAP) * (NCAP * cuts) + slot % NCAP)
    for cs in range(cuts):
        perm = (row == cs * NCAP).astype(F32).astype(BF)
        neg_ref[:, cs * LANES : (cs + 1) * LANES] = nn(perm, con).astype(BF)
    tq = tq_ref[...]
    prob = jax.nn.sigmoid(nt(tq, neg_ref[...]))
    an = (negative_weight * n_ref[:, :1] * prob).astype(BF)
    an_ref[...] = an
    dneg = tn(an, tq).astype(BF)
    wide = dneg_ref.shape[1]
    for cs in range(width // wide):
        dneg_ref[cs * slots : (cs + 1) * slots, :] = dneg[:, cs * wide : (cs + 1) * wide]


def head_kernel(at_ref, an_ref, par_ref, neg_ref, rel_ref, tail_ref, g_ref, out_ref):
    rows = par_ref.shape[0]
    kinds = rel_ref.shape[0]
    g = (nn(at_ref[...], par_ref[...]) + nn(an_ref[...], neg_ref[...])).astype(BF)
    g_ref[...] = g
    total = tail_ref[...].astype(F32)
    for t in range(kinds):
        total = total + nt(g[t * rows : (t + 1) * rows], rel_ref[t])
    wide = out_ref.shape[2]
    for cs in range(out_ref.shape[0]):
        out_ref[cs] = total[:, cs * wide : (cs + 1) * wide].astype(BF)


def rel_kernel(first, *refs):
    ent_ref, g_ref = refs[:2]
    out_ref = refs[-1]
    rows = ent_ref.shape[0]
    ent = ent_ref[...]
    for t in range(out_ref.shape[0]):
        part = tn(ent, g_ref[t * rows : (t + 1) * rows])
        if not first:
            part = part + refs[2][t]
        out_ref[t] = part.astype(out_ref.dtype)


def join_kernel(parts_ref, neg_ref, idx_ref, out_ref):
    rows = parts_ref.shape[1]
    total = nn(one_hot_rows(rows, idx_ref[...]), neg_ref[...])
    for j in range(parts_ref.shape[0]):
        total = total + parts_ref[j].astype(F32)
    total = total.astype(BF)
    for j in range(out_ref.shape[0]):
        out_ref[j] = total


def update(grad_ref, ent_ref, acc_ref, new_ref, new_acc_ref):
    cuts, _, wide = grad_ref.shape
    grads = [grad_ref[j].astype(F32) for j in range(cuts)]
    square = sum(jnp.sum(g * g, axis=-1, keepdims=True) for g in grads)
    acc = acc_ref[...] + square / (cuts * wide)
    new_acc_ref[...] = acc
    scale = entity_rate / jnp.sqrt(acc)
    for j in range(cuts):
        cut = slice(j * wide, (j + 1) * wide)
        new_ref[:, cut] = ent_ref[:, cut] - scale * grads[j]


def update_kernel(grad_ref, ent_ref, acc_ref, idx_ref, new_ref, new_acc_ref, bf_ref, con_ref):
    update(grad_ref, ent_ref, acc_ref, new_ref, new_acc_ref)
    bf = new_ref[...].astype(BF)
    bf_ref[...] = bf
    fill_container(con_ref, bf, idx_ref[...])


def total_kernel(parts_ref, out_ref):
    total = jnp.sum(parts_ref[...].astype(F32), axis=0).astype(BF)
    out_ref[...] = jnp.broadcast_to(total[None], out_ref.shape)


def on_device(entities, ent_accum, relations, rel_accum, heads, tails, relation_ids, negatives):
    rows, width = entities.shape
    parts = lax.axis_size("dom")
    reps = lax.axis_size("rep")
    kinds = relations.shape[0]
    slots = parts * NCAP
    wide = width // reps
    cuts = width // LANES
    everyone = ("rep", "dom")
    mine = lax.axis_index("rep")

    asked = negatives.reshape(ROUNDS, parts, NCAP).transpose(1, 0, 2).reshape(1, parts, ROUNDS * NCAP)
    asked = jnp.broadcast_to(asked, (reps, parts, ROUNDS * NCAP)).reshape(reps * parts, ROUNDS * NCAP)
    asked = all_ways(asked, everyone).reshape(reps, parts, ROUNDS, NCAP)
    served_all = asked.transpose(2, 0, 1, 3).reshape(ROUNDS, 1, reps * slots)
    own = lax.dynamic_index_in_dim(asked, mine, 0, keepdims=False).transpose(1, 0, 2)
    own = jnp.broadcast_to(own[:, :, None, :], (ROUNDS, parts, cuts, NCAP)).reshape(
        ROUNDS, 1, parts * cuts * NCAP
    )

    rel_bf = relations.astype(BF)
    ent_bf = entities.astype(BF)
    accum = ent_accum.reshape(rows, 1)
    con = None
    drel = None
    for rnd in range(ROUNDS):
        offset = rnd + 1
        last = rnd == ROUNDS - 1
        if rnd == 0:
            (con,) = call(serve_kernel, [((parts * cuts * NCAP, LANES), BF)], ent_bf, own[0])
        partner = from_behind(ent_bf, "dom", -offset)
        con = all_ways(con.reshape(parts, cuts * NCAP, LANES), "dom").reshape(parts * cuts * NCAP, LANES)
        tq, at, n, dtail = call(
            tail_kernel,
            [((kinds * rows, width), BF), ((kinds * rows, rows), BF), ((kinds * rows, LANES), F32), ((rows, width), BF)],
            ent_bf,
            rel_bf,
            partner,
            heads[rnd : rnd + 1],
            tails[rnd : rnd + 1],
            relation_ids[rnd : rnd + 1],
        )
        dtail = from_behind(dtail, "dom", offset)
        neg, an, dneg = call(
            neg_kernel,
            [((slots, width), BF), ((kinds * rows, slots), BF), ((reps * slots, wide), BF)],
            con,
            tq,
            n,
        )
        dneg = all_ways(dneg.reshape(reps * parts, NCAP, wide), everyone).reshape(reps * slots, wide)
        g, dhead = call(
            head_kernel,
            [((kinds * rows, width), BF), ((reps, rows, wide), BF)],
            at,
            an,
            partner,
            neg,
            rel_bf,
            dtail,
        )
        dhead = all_ways(dhead, "rep")
        args = (ent_bf, g) if rnd == 0 else (ent_bf, g, drel)
        (drel,) = call(
            lambda *refs, first=rnd == 0: rel_kernel(first, *refs),
            [((kinds, width, width), BF if last else F32)],
            *args,
            aliases={2: 0} if rnd > 0 and not last else None,
        )
        (grads,) = call(join_kernel, [((reps, rows, wide), BF)], dhead, dneg, served_all[rnd])
        grads = all_ways(grads, "rep")
        if last:
            entities, accum = call(update, [((rows, width), F32), ((rows, 1), F32)], grads, entities, accum)
        else:
            entities, accum, ent_bf, con = call(
                update_kernel,
                [((rows, width), F32), ((rows, 1), F32), ((rows, width), BF), ((parts * cuts * NCAP, LANES), BF)],
                grads,
                entities,
                accum,
                own[rnd + 1],
            )
    piece = kinds * width // parts
    drel = all_ways(drel.reshape(parts, piece, width), "dom")
    (total,) = call(total_kernel, [((parts, piece, width), BF)], drel)
    total = all_ways(total, "dom").reshape(kinds, width, width).astype(F32)
    new_rel_accum = rel_accum + total * total
    new_relations = relations - relation_rate * total / jnp.sqrt(new_rel_accum)
    return (entities, accum.reshape(rows), new_relations, new_rel_accum)


def solution(mesh):
    in_specs = (
        P("dom", None),
        P("dom"),
        P("rep", None, None),
        P("rep", None, None),
        P(None, ("dom", "rep")),
        P(None, ("dom", "rep")),
        P(None, ("dom", "rep")),
        P(None, ("dom", "rep")),
    )
    out_specs = (P("dom", None), P("dom"), P("rep", None, None), P("rep", None, None))
    return jax.shard_map(
        on_device, mesh=mesh, in_specs=in_specs, out_specs=out_specs, check_vma=False
    )
```

```python
import functools

import jax
import jax.numpy as jnp
from jax import lax
from jax.experimental import pallas as pl
from jax.experimental.pallas import tpu as pltpu
from jax.sharding import PartitionSpec as P


NCAP = 4
ROUNDS = 3
LANES = 128

negative_weight = 0.0625
entity_rate = 0.05
relation_rate = 0.02

BF = jnp.bfloat16
F32 = jnp.float32


class Late:
    def __init__(self, source, target, buffer, sem):
        self.copy = pltpu.make_async_copy(source, target, sem)
        self.buffer = buffer

    def ready(self):
        self.copy.wait()
        return self.buffer

    def send(self):
        self.copy.start()


def call(kernel, outs, *args, late=(), far=(), scratch=(), vmem=60 * 1024):
    outs = [jax.ShapeDtypeStruct(s, d) for s, d in outs]
    moved = sum(a.size * a.dtype.itemsize for a in args)
    moved += sum(o.size * o.dtype.itemsize for o in outs)
    near = pl.BlockSpec(memory_space=pltpu.VMEM)
    hbm = pl.BlockSpec(memory_space=pltpu.HBM)
    count = len(late) + len(far)
    buffers = [pltpu.VMEM(args[i].shape, args[i].dtype) for i in late]
    buffers += [pltpu.VMEM(outs[i].shape, outs[i].dtype) for i in far]
    sems = [pltpu.SemaphoreType.DMA((count,))] if count else []

    def body(*refs):
        refs = list(refs)
        sem = refs.pop() if count else None
        bufs = refs[len(refs) - count :]
        refs = refs[: len(refs) - count]
        for b, i in enumerate(late):
            refs[i] = Late(refs[i], bufs[b], bufs[b], sem.at[b])
            refs[i].send()
        sent = []
        for b, i in enumerate(far, len(late)):
            i += len(args)
            refs[i] = Late(bufs[b], refs[i], bufs[b], sem.at[b])
            sent.append(refs[i])
        kernel(*refs)
        for item in sent:
            item.ready()

    return pl.pallas_call(
        body,
        out_shape=outs,
        in_specs=[hbm if i in late else near for i in range(len(args))],
        out_specs=[hbm if i in far else near for i in range(len(outs))],
        scratch_shapes=list(scratch) + buffers + sems,
        compiler_params=pltpu.CompilerParams(vmem_limit_bytes=vmem << 10),
        cost_estimate=pl.CostEstimate(flops=0, bytes_accessed=moved, transcendentals=0),
    )(*args)


def nn(a, b):
    return jnp.dot(a, b, preferred_element_type=F32)


def nt(a, b):
    return lax.dot_general(a, b, (((1,), (1,)), ((), ())), preferred_element_type=F32)


def tn(a, b):
    return lax.dot_general(a, b, (((0,), (0,)), ((), ())), preferred_element_type=F32)


def iota(shape, dim):
    return lax.broadcasted_iota(jnp.int32, shape, dim)


def one_hot_rows(count, index):
    return (iota((count, index.shape[1]), 0) == index).astype(F32).astype(BF)


def all_ways(block, axes):
    return lax.all_to_all(block, axes, split_axis=0, concat_axis=0, tiled=True)


def from_behind(block, axis, distance):
    n = lax.axis_size(axis)
    return lax.ppermute(block, axis, [((i - distance) % n, i) for i in range(n)])


def fill_container(out_ref, ent_bf, idx_x):
    width = ent_bf.shape[1]
    cuts = width // LANES
    picked = tn(one_hot_rows(ent_bf.shape[0], idx_x), ent_bf)
    which = (iota((idx_x.shape[1], LANES), 0) // NCAP) % cuts
    out = picked[:, :LANES]
    for cs in range(1, cuts):
        out = jnp.where(which == cs, picked[:, cs * LANES : (cs + 1) * LANES], out)
    out_ref[...] = out.astype(BF)


def serve_kernel(ent_ref, idx_ref, out_ref):
    fill_container(out_ref, ent_ref[...], idx_ref[:1])


def tail_kernel(rnd, ent_ref, rel_ref, par_ref, head_ref, tail_ref, kind_ref, tq_ref, at_ref, n_ref, dtail_ref):
    rows = ent_ref.shape[0]
    kinds = rel_ref.buffer.shape[0]
    now = slice(rnd, rnd + 1)
    pick_q = one_hot_rows(kinds * rows, kind_ref[now] * rows + head_ref[now])
    pick_t = one_hot_rows(rows, tail_ref[now])
    ones = jnp.ones((LANES, pick_q.shape[1]), F32).astype(BF)
    joint = nt(pick_t, pick_q)
    n = nt(ones[:8], pick_q)
    c = nt(pick_t, ones)
    n_ref[...] = n
    rel = rel_ref.ready()
    ent = ent_ref[...]
    for t in range(kinds):
        tq_ref[t * rows : (t + 1) * rows, :] = nn(ent, rel[t]).astype(BF)
    tq = tq_ref[...]
    prob = jax.nn.sigmoid(nt(par_ref[...], tq))
    weight = (negative_weight * c[:, :1]) * n[:1]
    at = (weight * prob + joint * ((1.0 - negative_weight) * prob - 1.0)).astype(BF)
    at_ref[...] = at
    dtail_ref[...] = nn(at, tq).astype(BF)


def neg_kernel(con_ref, tq_ref, n_ref, neg_ref, an_ref, dneg_ref):
    slots, width = neg_ref.shape
    cuts = width // LANES
    con = con_ref[...]
    slot = iota((slots, con.shape[0]), 0)
    row = iota((slots, con.shape[0]), 1) - ((slot // NCAP) * (NCAP * cuts) + slot % NCAP)
    for cs in range(cuts):
        perm = (row == cs * NCAP).astype(F32).astype(BF)
        neg_ref[:, cs * LANES : (cs + 1) * LANES] = nn(perm, con).astype(BF)
    tq = tq_ref[...]
    prob = jax.nn.sigmoid(nt(neg_ref[...], tq))
    an = (negative_weight * n_ref[:1] * prob).astype(BF)
    an_ref[...] = an
    dneg = nn(an, tq).astype(BF)
    wide = dneg_ref.shape[1]
    for cs in range(width // wide):
        dneg_ref[cs * slots : (cs + 1) * slots, :] = dneg[:, cs * wide : (cs + 1) * wide]


def head_kernel(at_ref, an_ref, par_ref, neg_ref, rel_ref, tail_ref, keep_ref, *refs):
    out_refs, cut_ref = refs[:-1], refs[-1]
    reps = len(out_refs)
    rows = par_ref.shape[0]
    g_ref = keep_ref.buffer
    g_ref[...] = (tn(at_ref[...], par_ref[...]) + tn(an_ref[...], neg_ref[...])).astype(BF)
    keep_ref.send()
    total = tail_ref[...].astype(F32)
    rel = rel_ref.ready()
    for t in range(rel.shape[0]):
        total = total + nt(g_ref[t * rows : (t + 1) * rows, :], rel[t])
    wide = cut_ref.shape[2]
    for cs in range(reps):
        cut_ref[cs] = total[:, cs * wide : (cs + 1) * wide].astype(BF)
    mine = lax.axis_index("rep")
    for s in range(reps):
        out_refs[s][...] = cut_ref[lax.rem(mine + s, reps)]


def rel_kernel(*refs):
    refs = [ref.ready() for ref in refs[: 2 * ROUNDS]] + list(refs[2 * ROUNDS :])
    ents = [ref[...].astype(BF) for ref in refs[:ROUNDS]]
    g_refs, (given_ref, kept_ref) = refs[ROUNDS : 2 * ROUNDS], refs[2 * ROUNDS :]
    rows = ents[0].shape[0]
    core = lax.rem(lax.axis_index("dom"), 2)

    def half(which):
        cut = pl.ds(pl.multiple_of(which * rows, rows), rows)
        return sum(tn(ent, g_ref[cut, :]) for ent, g_ref in zip(ents, g_refs))

    kept_ref.buffer[...] = half(core)
    kept_ref.send()
    given_ref[...] = half(1 - core).astype(BF)


def pair_kernel(kept_ref, got_ref, out_ref):
    out_ref[...] = (kept_ref.ready()[...] + got_ref[...].astype(F32)).astype(BF)


def join_kernel(rnd, neg_ref, *refs):
    out_ref = refs[-1]
    reps = len(refs) // 2
    idx_refs, part_refs = refs[:reps], refs[reps:-1]
    rows = out_ref.shape[0]
    mine = lax.axis_index("rep")
    slots = idx_refs[0].shape[1]
    total = part_refs[0][...].astype(F32)
    for part_ref in part_refs[1:]:
        total = total + part_ref[...].astype(F32)
    for s, idx_ref in enumerate(idx_refs):
        start = pl.multiple_of(lax.rem(mine + s, reps) * slots, slots)
        total = total + nn(one_hot_rows(rows, idx_ref[rnd : rnd + 1]), neg_ref[pl.ds(start, slots), :])
    out_ref[...] = total.astype(BF)


def update(part_refs, ent_ref, acc_ref, new_ref, new_acc_ref, grad_ref):
    reps, _, wide = grad_ref.shape
    mine = lax.axis_index("rep")
    for s, part_ref in enumerate(part_refs):
        grad_ref[lax.rem(mine + s, reps)] = part_ref[...].astype(F32)
    grads = [grad_ref[j] for j in range(reps)]
    square = sum(jnp.sum(g * g, axis=-1, keepdims=True) for g in grads)
    acc = acc_ref[...] + square / (reps * wide)
    new_acc_ref[...] = acc
    scale = entity_rate / jnp.sqrt(acc)
    ent = ent_ref.ready()
    for j in range(reps):
        cut = slice(j * wide, (j + 1) * wide)
        new_ref.buffer[:, cut] = ent[:, cut] - scale * grads[j]
    new_ref.send()


def last_update_kernel(*refs):
    update(refs[:-5], *refs[-5:])


def update_kernel(rnd, *refs):
    part_refs = refs[:-9]
    ent_ref, acc_ref, idx_ref, new_acc_ref, bf_ref, con_ref, new_ref, keep_ref, grad_ref = refs[-9:]
    update(part_refs, ent_ref, acc_ref, new_ref, new_acc_ref, grad_ref)
    bf = new_ref.buffer[...].astype(BF)
    bf_ref[...] = bf
    keep_ref.buffer[...] = bf
    keep_ref.send()
    fill_container(con_ref, bf, idx_ref[rnd + 1 : rnd + 2])


def total_kernel(parts_ref, out_ref):
    parts, piece, width = parts_ref.shape
    pairs = parts_ref[...].reshape(parts // 2, 2, piece, width)
    total = jnp.sum(pairs.astype(F32), axis=0).astype(BF)
    out_ref[...] = jnp.broadcast_to(total[None], pairs.shape).reshape(parts, piece, width)


def final_kernel(which_ref, total_ref, rel_ref, acc_ref, *refs):
    new_ref, new_acc_ref = refs[-2:]
    total = total_ref[...].astype(F32)
    acc = acc_ref[...] + total * total
    new_acc_ref[...] = acc
    new_ref[...] = rel_ref[...] - relation_rate * total * lax.rsqrt(acc)


def final_update(which, total, relations, rel_accum, out):
    width = total.shape[0]
    block = width // 4
    slab = pl.BlockSpec((None, block, width), lambda i, which_ref: (which_ref[0], i, 0))
    return pl.pallas_call(
        final_kernel,
        grid_spec=pltpu.PrefetchScalarGridSpec(
            num_scalar_prefetch=1,
            grid=(width // block,),
            in_specs=[pl.BlockSpec((block, width), lambda i, which_ref: (i, 0)), slab, slab]
            + [pl.BlockSpec(memory_space=pltpu.HBM)] * len(out),
            out_specs=[slab, slab],
        ),
        out_shape=[jax.ShapeDtypeStruct(relations.shape, F32)] * 2,
        input_output_aliases={4 + i: i for i in range(len(out))},
        compiler_params=pltpu.CompilerParams(vmem_limit_bytes=60 * 1024 * 1024),
        cost_estimate=pl.CostEstimate(flops=0, bytes_accessed=17 * width * width, transcendentals=0),
    )(which, total, relations, rel_accum, *out)


def step(entities, ent_accum, relations, rel_accum, heads, tails, relation_ids, negatives):
    rows, width = entities.shape
    parts = lax.axis_size("dom")
    reps = lax.axis_size("rep")
    kinds = relations.shape[0]
    slots = parts * NCAP
    wide = width // reps
    cuts = width // LANES
    everyone = ("rep", "dom")

    asked = negatives.reshape(ROUNDS, parts, NCAP).transpose(1, 0, 2).reshape(parts, ROUNDS * NCAP)
    asked = all_ways(asked, "dom").reshape(parts, ROUNDS, NCAP).transpose(1, 0, 2)
    own = jnp.broadcast_to(asked[:, :, None, :], (ROUNDS, parts, cuts, NCAP)).reshape(
        ROUNDS, parts * cuts * NCAP
    )
    asked = asked.reshape(ROUNDS, slots)

    served = [asked]
    for s in range(1, reps):
        served.append(from_behind(asked, "rep", -s))

    rel_bf = relations.astype(BF)
    ent_bf = entities.astype(BF)
    accum = ent_accum.reshape(rows, 1)
    (con,) = call(serve_kernel, [((parts * cuts * NCAP, LANES), BF)], ent_bf, own)
    ents, gs = [entities], []
    for rnd in range(ROUNDS):
        offset = rnd + 1
        last = rnd == ROUNDS - 1
        partner = from_behind(ent_bf, "dom", -offset)
        con = all_ways(con.reshape(parts, cuts * NCAP, LANES), "dom").reshape(parts * cuts * NCAP, LANES)
        tq, at, n, dtail = call(
            functools.partial(tail_kernel, rnd),
            [((kinds * rows, width), BF), ((rows, kinds * rows), BF), ((8, kinds * rows), F32), ((rows, width), BF)],
            ent_bf,
            rel_bf,
            partner,
            heads,
            tails,
            relation_ids,
            late=(1,),
        )
        dtail = from_behind(dtail, "dom", offset)
        neg, an, dneg = call(
            neg_kernel,
            [((slots, width), BF), ((slots, kinds * rows), BF), ((reps * slots, wide), BF)],
            con,
            tq,
            n,
        )
        dneg = all_ways(dneg.reshape(reps * parts, NCAP, wide), everyone).reshape(reps * slots, wide)
        g, *dhead = call(
            head_kernel,
            [((kinds * rows, width), BF)] + [((rows, wide), BF)] * reps,
            at,
            an,
            partner,
            neg,
            rel_bf,
            dtail,
            late=(4,),
            far=(0,),
            scratch=[pltpu.VMEM((reps, rows, wide), BF)],
        )
        gs.append(g)
        for s in range(1, reps):
            dhead[s] = from_behind(dhead[s], "rep", s)
        (grads,) = call(functools.partial(join_kernel, rnd), [((rows, wide), BF)], dneg, *served, *dhead)
        parts_of = [grads]
        for s in range(1, reps):
            parts_of.append(from_behind(grads, "rep", -s))
        grad_scratch = pltpu.VMEM((reps, rows, wide), F32)
        if last:
            accum, entities = call(
                lambda *refs: last_update_kernel(*refs[:-3], refs[-2], refs[-3], refs[-1]),
                [((rows, 1), F32), ((rows, width), F32)],
                *parts_of,
                entities,
                accum,
                late=(reps,),
                far=(1,),
                scratch=[grad_scratch],
            )
        else:
            accum, ent_bf, con, entities, keep = call(
                functools.partial(update_kernel, rnd),
                [
                    ((rows, 1), F32),
                    ((rows, width), BF),
                    ((parts * cuts * NCAP, LANES), BF),
                    ((rows, width), F32),
                    ((rows, width), BF),
                ],
                *parts_of,
                entities,
                accum,
                own,
                late=(reps,),
                far=(3, 4),
                scratch=[grad_scratch],
            )
            ents.append(keep)
    pair = [(i ^ 1, i) for i in range(parts)]
    given, kept = call(
        rel_kernel,
        [((width, width), BF), ((width, width), F32)],
        *ents,
        *gs,
        late=tuple(range(2 * ROUNDS)),
        far=(1,),
    )
    got = lax.ppermute(given, "dom", pair)
    (drel,) = call(pair_kernel, [((width, width), BF)], kept, got, late=(0,))
    piece = width // parts
    drel = all_ways(drel.reshape(parts, piece, width), "dom")
    (total,) = call(total_kernel, [((parts, piece, width), BF)], drel)
    total = all_ways(total, "dom").reshape(width, width)
    other = lax.ppermute(total, "dom", pair)
    core = lax.rem(lax.axis_index("dom"), 2).reshape(1)
    out = final_update(core, total, relations, rel_accum, ())
    out = final_update(1 - core, other, relations, rel_accum, out)
    return (entities, accum.reshape(rows), *out)


def solution(mesh):
    in_specs = (
        P("dom", None),
        P("dom"),
        P("rep", None, None),
        P("rep", None, None),
        P(None, ("dom", "rep")),
        P(None, ("dom", "rep")),
        P(None, ("dom", "rep")),
        P(None, ("dom", "rep")),
    )
    out_specs = (P("dom", None), P("dom"), P("rep", None, None), P("rep", None, None))
    return jax.shard_map(step, mesh=mesh, in_specs=in_specs, out_specs=out_specs, check_vma=False)
```

```python
import functools
import math

import jax
import jax.numpy as jnp
from jax import lax
from jax.experimental import pallas as pl
from jax.experimental.pallas import tpu as pltpu
from jax.sharding import PartitionSpec as P


NCAP = 4
ROUNDS = 3
LANES = 128
INDEX_LINES = 16
FAR = 4 << 20

negative_weight = 0.0625
entity_rate = 0.05
relation_rate = 0.02

BF = jnp.bfloat16
F32 = jnp.float32


class Late:
    def __init__(self, source, target, buffer, sem):
        self.copy = pltpu.make_async_copy(source, target, sem)
        self.buffer = buffer

    def ready(self):
        self.copy.wait()
        return self.buffer

    def send(self):
        self.copy.start()


def call(kernel, outs, *args, late=None, far=(), scratch=(), vmem=53500):
    late = late or {}
    shapes = []
    for i, (shape, dtype) in enumerate(outs):
        whole = shape
        if i in far:
            row = math.prod(shape[1:]) * jnp.dtype(dtype).itemsize
            whole = (max(shape[0], FAR // row),) + tuple(shape[1:])
        shapes.append(jax.ShapeDtypeStruct(whole, dtype))
    moved = sum(math.prod(shape) * jnp.dtype(dtype).itemsize for shape, dtype in outs)
    moved += sum((a.size if i not in late else a.size // a.shape[0] * late[i]) * a.dtype.itemsize for i, a in enumerate(args))
    near = pl.BlockSpec(memory_space=pltpu.VMEM)
    hbm = pl.BlockSpec(memory_space=pltpu.HBM)
    count = len(late) + len(far)
    buffers = [pltpu.VMEM((late[i],) + args[i].shape[1:], args[i].dtype) for i in late]
    buffers += [pltpu.VMEM(*outs[i]) for i in far]
    sems = [pltpu.SemaphoreType.DMA((count,))] if count else []

    def body(*refs):
        refs = list(refs)
        sem = refs.pop() if count else None
        bufs = refs[len(refs) - count :]
        refs = refs[: len(refs) - count]
        for b, i in enumerate(late):
            refs[i] = Late(refs[i].at[: late[i]], bufs[b], bufs[b], sem.at[b])
            refs[i].send()
        sent = []
        for b, i in enumerate(far, len(late)):
            out = refs[len(args) + i].at[: outs[i][0][0]]
            refs[len(args) + i] = Late(bufs[b], out, bufs[b], sem.at[b])
            sent.append(refs[len(args) + i])
        kernel(*refs)
        for item in sent:
            item.ready()

    return pl.pallas_call(
        body,
        out_shape=shapes,
        in_specs=[hbm if i in late else near for i in range(len(args))],
        out_specs=[hbm if i in far else near for i in range(len(outs))],
        scratch_shapes=list(scratch) + buffers + sems,
        compiler_params=pltpu.CompilerParams(vmem_limit_bytes=vmem << 10),
        cost_estimate=pl.CostEstimate(flops=0, bytes_accessed=moved, transcendentals=0),
    )(*args)


def nn(a, b):
    return jnp.dot(a, b, preferred_element_type=F32)


def nt(a, b):
    return lax.dot_general(a, b, (((1,), (1,)), ((), ())), preferred_element_type=F32)


def tn(a, b):
    return lax.dot_general(a, b, (((0,), (0,)), ((), ())), preferred_element_type=F32)


def iota(shape, dim):
    return lax.broadcasted_iota(jnp.int32, shape, dim)


def one_hot_rows(count, index):
    return (iota((count, index.shape[1]), 0) == index).astype(F32).astype(BF)


def all_ways(block, axes):
    return lax.all_to_all(block, axes, split_axis=0, concat_axis=0, tiled=True)


def from_behind(block, axis, distance):
    n = lax.axis_size(axis)
    return lax.ppermute(block, axis, [((i - distance) % n, i) for i in range(n)])


def fill_container(out_ref, sel_ref, ent_ref, idx_ref, rnd):
    rows, width = ent_ref.shape
    cuts = width // LANES
    sel_ref[...] = tn(one_hot_rows(rows, idx_ref[rnd : rnd + 1]), ent_ref[...]).astype(BF)
    slots = sel_ref.shape[0]
    block = out_ref.shape[0] // cuts
    line = iota((block, slots), 0)
    which = (line // NCAP) % cuts
    slot = line // (NCAP * cuts) * NCAP + line % NCAP - iota((block, slots), 1)

    @pl.loop(0, cuts)
    def _(i):
        first = i * (block // cuts)
        out = jnp.zeros((block, LANES), F32)
        for cs in range(cuts):
            perm = ((slot + first == 0) & (which == cs)).astype(F32).astype(BF)
            out = out + nn(perm, sel_ref[:, cs * LANES : (cs + 1) * LANES])
        out_ref[pl.ds(pl.multiple_of(i * block, block), block), :] = out.astype(BF)


def round_kernel(in_ref, out_ref):
    out_ref.buffer[...] = in_ref.ready()[...].astype(BF)
    out_ref.send()


def serve_kernel(ent_ref, idx_ref, out_ref, sel_ref):
    fill_container(out_ref, sel_ref, ent_ref, idx_ref, 0)


def tail_kernel(rnd, ent_ref, rel_ref, par_ref, head_ref, tail_ref, kind_ref, tq_ref, at_ref, n_ref, dtail_ref, pick_ref):
    rows = ent_ref.shape[0]
    kinds = rel_ref.buffer.shape[0]
    now = slice(rnd, rnd + 1)
    pick_ref[...] = one_hot_rows(kinds * rows, kind_ref[now] * rows + head_ref[now])
    tail = tail_ref[now]
    ones = jnp.ones((8, tail.shape[1]), F32).astype(BF)
    n = nt(ones, pick_ref[...])
    n_ref[...] = n
    rel = rel_ref.ready()

    @pl.loop(0, kinds)
    def _(t):
        cut = pl.ds(pl.multiple_of(t * rows, rows), rows)
        tq_ref[cut, :] = nn(ent_ref[...], rel[t]).astype(BF)

    block = rows // 2

    @pl.loop(0, 2)
    def _(i):
        cut = pl.ds(pl.multiple_of(i * block, block), block)
        pick_t = iota((block, tail.shape[1]), 0) + i * block == tail
        c = jnp.sum(pick_t.astype(F32), axis=1, keepdims=True)
        joint = nt(pick_t.astype(F32).astype(BF), pick_ref[...])
        prob = jax.nn.sigmoid(nt(par_ref[cut, :], tq_ref[...]))
        weight = (negative_weight * c) * n[:1]
        at = (weight * prob + joint * ((1.0 - negative_weight) * prob - 1.0)).astype(BF)
        at_ref[cut, :] = at
        dtail_ref[cut, :] = nn(at, tq_ref[...]).astype(BF)


def main_kernel(con_ref, tq_ref, n_ref, at_ref, par_ref, rel_ref, tail_ref, *refs):
    neg_ref, an_ref, sum_ref, cut_ref = refs[-4:]
    dneg_ref, g_ref = refs[0], refs[-5]
    out_refs = refs[1:-5]
    slots, width = neg_ref.shape
    cuts = width // LANES
    kinds = rel_ref.buffer.shape[0]
    rows = par_ref.shape[0]
    reps = cut_ref.shape[0]
    idx_ref = None
    if len(out_refs) > reps:
        idx_ref, out_refs = out_refs[0], out_refs[1:]
        dneg_ref, idx_ref = idx_ref, dneg_ref
    slot = iota((slots, con_ref.shape[0]), 0)
    row = iota((slots, con_ref.shape[0]), 1) - ((slot // NCAP) * (NCAP * cuts) + slot % NCAP)

    @pl.loop(0, cuts)
    def _(cs):
        perm = (row == cs * NCAP).astype(F32).astype(BF)
        cut = pl.ds(pl.multiple_of(cs * LANES, LANES), LANES)
        neg_ref[:, cut] = nn(perm, con_ref[...]).astype(BF)

    wide = dneg_ref.shape[1]
    block = slots // 2

    @pl.loop(0, 2)
    def _(i):
        cut = pl.ds(pl.multiple_of(i * block, block), block)
        prob = jax.nn.sigmoid(nt(neg_ref[cut, :], tq_ref[...]))
        an = (negative_weight * n_ref[:1] * prob).astype(BF)
        an_ref[cut, :] = an
        dneg = nn(an, tq_ref[...]).astype(BF)
        for cs in range(width // wide):
            start = pl.multiple_of(cs * slots + i * block, block)
            dneg_ref[pl.ds(start, block), :] = dneg[:, cs * wide : (cs + 1) * wide]

    rel = rel_ref.ready()
    sum_ref[...] = tail_ref[...].astype(F32)

    half = rows // 2

    @pl.loop(0, 2 * kinds)
    def _(i):
        cut = pl.ds(pl.multiple_of(i * half, half), half)
        g = (tn(at_ref[:, cut], par_ref[...]) + tn(an_ref[:, cut], neg_ref[...])).astype(BF)
        g_ref.buffer[cut, :] = g
        head = pl.ds(pl.multiple_of(i % 2 * half, half), half)
        sum_ref[head, :] += nt(g, rel[i // 2])

    g_ref.send()
    for cs in range(reps):
        cut_ref[cs] = sum_ref[:, cs * wide : (cs + 1) * wide].astype(BF)
    mine = lax.axis_index("rep")
    for s in range(reps):
        out_refs[s][:rows, :] = cut_ref[lax.rem(mine + s, reps)]
        if idx_ref is not None:
            out_refs[s][rows:, :] = idx_ref[...]


def rel_kernel(*refs):
    given_ref, kept_ref, ents_ref = refs[2 * ROUNDS :]
    rows, width = ents_ref.shape[1:]
    for r in range(ROUNDS):
        ents_ref[r] = refs[r].ready()[...].astype(BF)
    g_refs = [ref.ready() for ref in refs[ROUNDS : 2 * ROUNDS]]
    core = lax.rem(lax.axis_index("dom"), 2)
    block = width // 4

    def half(which, out_ref):
        cut = pl.ds(pl.multiple_of(which * rows, rows), rows)

        @pl.loop(0, 4)
        def _(i):
            part = pl.ds(pl.multiple_of(i * block, block), block)
            total = sum(tn(ents_ref[r, :, part], g_refs[r][cut, :]) for r in range(ROUNDS))
            out_ref[part, :] = total.astype(out_ref.dtype)

    half(core, kept_ref.buffer)
    kept_ref.send()
    half(1 - core, given_ref)


def pair_kernel(kept_ref, got_ref, out_ref):
    out_ref[...] = (kept_ref.ready()[...] + got_ref[...].astype(F32)).astype(BF)


def join_kernel(rnd, neg_ref, *refs):
    reps = (len(refs) - 1) // 2
    part_refs, idx_refs, out_refs = refs[:reps], refs[reps : 2 * reps], refs[2 * reps :]
    out_ref = out_refs[0]
    rows = out_ref.shape[1]
    slots = neg_ref.shape[0] // reps
    lines = slots // LANES
    mine = lax.axis_index("rep")
    total = part_refs[0][:rows, :].astype(F32)
    for part_ref in part_refs[1:]:
        total = total + part_ref[:rows, :].astype(F32)
    for s, idx_ref in enumerate(idx_refs):
        first = idx_ref.shape[0] - INDEX_LINES + rnd * lines
        for line in range(lines):
            start = lax.rem(mine + reps - s, reps) * slots + line * LANES
            index = idx_ref[first + line : first + line + 1, :].astype(F32).astype(jnp.int32)
            total = total + nn(one_hot_rows(rows, index), neg_ref[pl.ds(pl.multiple_of(start, LANES), LANES), :])
    out_ref[...] = jnp.broadcast_to(total.astype(BF)[None], out_ref.shape)


def update(grad_ref, ent_ref, acc_ref, new_ref):
    reps, _, wide = grad_ref.shape
    grads = [grad_ref[j].astype(F32) for j in range(reps)]
    square = sum(jnp.sum(g * g, axis=-1, keepdims=True) for g in grads)
    acc = acc_ref[...] + square / (reps * wide)
    scale = entity_rate / jnp.sqrt(acc)
    ent = ent_ref.ready()
    for j in range(reps):
        cut = slice(j * wide, (j + 1) * wide)
        new_ref[:, cut] = ent[:, cut] - scale * grads[j]
    return acc


def last_update_kernel(*refs):
    ent_ref, acc_ref, new_ref, new_acc_ref, grad_ref = refs[-5:]
    reps = grad_ref.shape[0]
    mine = lax.axis_index("rep")
    for s, part_ref in enumerate(refs[:-5]):
        grad_ref[lax.rem(mine + s, reps)] = part_ref[...]
    acc = update(grad_ref, ent_ref, acc_ref, new_ref)
    new_acc_ref[...] = jnp.broadcast_to(acc, (acc.shape[0], LANES)).T[:8]


def update_kernel(rnd, grad_ref, ent_ref, acc_ref, idx_ref, new_acc_ref, bf_ref, con_ref, new_ref, keep_ref, sel_ref):
    new_acc_ref[...] = update(grad_ref, ent_ref, acc_ref, new_ref.buffer)
    new_ref.send()
    bf_ref[...] = new_ref.buffer[...].astype(BF)
    keep_ref.buffer[...] = bf_ref[...]
    keep_ref.send()
    fill_container(con_ref, sel_ref, bf_ref, idx_ref, rnd + 1)


def total_kernel(parts_ref, out_ref):
    parts, piece, width = parts_ref.shape
    pairs = parts_ref[...].reshape(parts // 2, 2, piece, width)
    total = jnp.sum(pairs.astype(F32), axis=0).astype(BF).reshape(2 * piece, width)
    out_ref[...] = jnp.broadcast_to(total[None], out_ref.shape)


def step(entities, ent_accum, relations, rel_accum, heads, tails, relation_ids, negatives):
    rows, width = entities.shape
    parts = lax.axis_size("dom")
    reps = lax.axis_size("rep")
    kinds = relations.shape[0]
    slots = parts * NCAP
    wide = width // reps
    cuts = width // LANES
    everyone = ("rep", "dom")

    asked = negatives.reshape(ROUNDS, parts, NCAP).transpose(1, 0, 2).reshape(parts, ROUNDS * NCAP)
    asked = all_ways(asked, "dom").reshape(parts, ROUNDS, NCAP).transpose(1, 0, 2)
    own = asked.reshape(ROUNDS, slots)
    asked = asked.reshape(ROUNDS * slots // LANES, LANES)
    asked = jnp.pad(asked, ((0, INDEX_LINES - asked.shape[0]), (0, 0))).astype(BF)

    ent_bf = entities.astype(BF)
    accum = ent_accum.reshape(rows, 1)
    chosen = pltpu.VMEM((slots, width), BF)
    (con,) = call(serve_kernel, [((parts * cuts * NCAP, LANES), BF)], ent_bf, own, scratch=[chosen])
    ents, gs = [entities], []
    (rel_bf,) = call(round_kernel, [(relations.shape, BF)], relations, late={0: kinds}, far=(0,))
    for rnd in range(ROUNDS):
        offset = rnd + 1
        last = rnd == ROUNDS - 1
        partner = from_behind(ent_bf, "dom", -offset)
        con = all_ways(con.reshape(parts, cuts * NCAP, LANES), "dom").reshape(parts * cuts * NCAP, LANES)
        tq, at, n, dtail = call(
            functools.partial(tail_kernel, rnd),
            [((kinds * rows, width), BF), ((rows, kinds * rows), BF), ((8, kinds * rows), F32), ((rows, width), BF)],
            ent_bf,
            rel_bf,
            partner,
            heads,
            tails,
            relation_ids,
            late={1: kinds},
            scratch=[pltpu.VMEM((kinds * rows, heads.shape[1]), BF)],
        )
        dtail = from_behind(dtail, "dom", offset)
        lines = 0 if rnd else INDEX_LINES
        dneg, *dhead, g = call(
            main_kernel,
            [((reps * slots, wide), BF)] + [((rows + lines, wide), BF)] * reps + [((kinds * rows, width), BF)],
            con,
            tq,
            n,
            at,
            partner,
            rel_bf,
            dtail,
            *([] if rnd else [asked]),
            late={5: kinds},
            far=(1 + reps,),
            scratch=[
                pltpu.VMEM((slots, width), BF),
                pltpu.VMEM((slots, kinds * rows), BF),
                pltpu.VMEM((rows, width), F32),
                pltpu.VMEM((reps, rows, wide), BF),
            ],
        )
        dneg = all_ways(dneg.reshape(reps * parts, NCAP, wide), everyone).reshape(reps * slots, wide)
        gs.append(g)
        for s in range(1, reps):
            dhead[s] = from_behind(dhead[s], "rep", s)
        if rnd == 0:
            served = dhead
        (grads,) = call(
            functools.partial(join_kernel, rnd), [((1 if last else reps, rows, wide), BF)], dneg, *dhead, *served
        )
        if rnd == 0:
            served = [part[rows:] for part in dhead]
        if last:
            parts_of = [grads[0]]
            for s in range(1, reps):
                parts_of.append(from_behind(grads[0], "rep", -s))
        else:
            grads = all_ways(grads, "rep")
        if last:
            entities, accum = call(
                last_update_kernel,
                [((rows, width), F32), ((8, rows), F32)],
                *parts_of,
                entities,
                accum,
                late={reps: rows},
                scratch=[pltpu.VMEM((reps, rows, wide), BF)],
            )
        else:
            accum, ent_bf, con, entities, keep = call(
                functools.partial(update_kernel, rnd),
                [
                    ((rows, 1), F32),
                    ((rows, width), BF),
                    ((parts * cuts * NCAP, LANES), BF),
                    ((rows, width), F32),
                    ((rows, width), BF),
                ],
                grads,
                entities,
                accum,
                own,
                late={1: rows},
                far=(3, 4),
                scratch=[chosen],
            )
            ents.append(keep)
    pair = [(i ^ 1, i) for i in range(parts)]
    given, kept = call(
        rel_kernel,
        [((width, width), BF), ((width, width), F32)],
        *ents,
        *gs,
        late={i: rows if i < ROUNDS else kinds * rows for i in range(2 * ROUNDS)},
        far=(1,),
        scratch=[pltpu.VMEM((ROUNDS, rows, width), BF)],
    )
    got = lax.ppermute(given, "dom", pair)
    (drel,) = call(pair_kernel, [((width, width), BF)], kept, got, late={0: width})
    piece = width // parts
    drel = all_ways(drel.reshape(parts, piece, width), "dom")
    (total,) = call(total_kernel, [((parts, kinds * piece, width), BF)], drel)
    total = all_ways(total, "dom")
    total = total.reshape(parts, kinds, piece, width).transpose(1, 0, 2, 3).reshape(kinds, width, width)
    total = total.astype(F32)
    new_rel_accum = rel_accum + total * total
    new_relations = relations - relation_rate * total * lax.rsqrt(new_rel_accum)
    return (entities, accum[0], new_relations, new_rel_accum)


def solution(mesh):
    in_specs = (
        P("dom", None),
        P("dom"),
        P("rep", None, None),
        P("rep", None, None),
        P(None, ("dom", "rep")),
        P(None, ("dom", "rep")),
        P(None, ("dom", "rep")),
        P(None, ("dom", "rep")),
    )
    out_specs = (P("dom", None), P("dom"), P("rep", None, None), P("rep", None, None))
    return jax.shard_map(step, mesh=mesh, in_specs=in_specs, out_specs=out_specs, check_vma=False)
```

```python
import functools
import math

import jax
import jax.numpy as jnp
from jax import lax
from jax.experimental import pallas as pl
from jax.experimental.pallas import tpu as pltpu
from jax.sharding import PartitionSpec as P


NCAP = 4
ROUNDS = 3
LANES = 128
INDEX_LINES = 16
FAR = 4 << 20

negative_weight = 0.0625
entity_rate = 0.05
relation_rate = 0.02

BF = jnp.bfloat16
F32 = jnp.float32


class Late:
    def __init__(self, source, target, buffer, sem):
        self.copy = pltpu.make_async_copy(source, target, sem)
        self.buffer = buffer

    def ready(self):
        self.copy.wait()
        return self.buffer

    def send(self):
        self.copy.start()


def call(kernel, outs, *args, late=None, far=(), scratch=(), vmem=53500):
    late = late or {}
    shapes = []
    for i, (shape, dtype) in enumerate(outs):
        whole = shape
        if i in far:
            row = math.prod(shape[1:]) * jnp.dtype(dtype).itemsize
            whole = (max(shape[0], FAR // row),) + tuple(shape[1:])
        shapes.append(jax.ShapeDtypeStruct(whole, dtype))
    moved = sum(math.prod(shape) * jnp.dtype(dtype).itemsize for shape, dtype in outs)
    moved += sum((a.size if i not in late else a.size // a.shape[0] * late[i]) * a.dtype.itemsize for i, a in enumerate(args))
    near = pl.BlockSpec(memory_space=pltpu.VMEM)
    hbm = pl.BlockSpec(memory_space=pltpu.HBM)
    count = len(late) + len(far)
    buffers = [pltpu.VMEM((late[i],) + args[i].shape[1:], args[i].dtype) for i in late]
    buffers += [pltpu.VMEM(*outs[i]) for i in far]
    sems = [pltpu.SemaphoreType.DMA((count,))] if count else []

    def body(*refs):
        refs = list(refs)
        sem = refs.pop() if count else None
        bufs = refs[len(refs) - count :]
        refs = refs[: len(refs) - count]
        for b, i in enumerate(late):
            refs[i] = Late(refs[i].at[: late[i]], bufs[b], bufs[b], sem.at[b])
            refs[i].send()
        sent = []
        for b, i in enumerate(far, len(late)):
            out = refs[len(args) + i].at[: outs[i][0][0]]
            refs[len(args) + i] = Late(bufs[b], out, bufs[b], sem.at[b])
            sent.append(refs[len(args) + i])
        kernel(*refs)
        for item in sent:
            item.ready()

    return pl.pallas_call(
        body,
        out_shape=shapes,
        in_specs=[hbm if i in late else near for i in range(len(args))],
        out_specs=[hbm if i in far else near for i in range(len(outs))],
        scratch_shapes=list(scratch) + buffers + sems,
        compiler_params=pltpu.CompilerParams(vmem_limit_bytes=vmem << 10),
        cost_estimate=pl.CostEstimate(flops=0, bytes_accessed=moved, transcendentals=0),
    )(*args)


def nn(a, b):
    return jnp.dot(a, b, preferred_element_type=F32)


def nt(a, b):
    return lax.dot_general(a, b, (((1,), (1,)), ((), ())), preferred_element_type=F32)


def tn(a, b):
    return lax.dot_general(a, b, (((0,), (0,)), ((), ())), preferred_element_type=F32)


def iota(shape, dim):
    return lax.broadcasted_iota(jnp.int32, shape, dim)


def one_hot_rows(count, index):
    return (iota((count, index.shape[1]), 0) == index).astype(F32).astype(BF)


def all_ways(block, axes):
    return lax.all_to_all(block, axes, split_axis=0, concat_axis=0, tiled=True)


def from_behind(block, axis, distance):
    n = lax.axis_size(axis)
    return lax.ppermute(block, axis, [((i - distance) % n, i) for i in range(n)])


def fill_container(out_ref, sel_ref, ent_ref, idx_ref, rnd):
    rows, width = ent_ref.shape
    cuts = width // LANES
    sel_ref[...] = tn(one_hot_rows(rows, idx_ref[rnd : rnd + 1]), ent_ref[...]).astype(BF)
    slots = sel_ref.shape[0]
    block = out_ref.shape[0] // cuts
    line = iota((block, slots), 0)
    which = (line // NCAP) % cuts
    slot = line // (NCAP * cuts) * NCAP + line % NCAP - iota((block, slots), 1)

    @pl.loop(0, cuts)
    def _(i):
        first = i * (block // cuts)
        out = jnp.zeros((block, LANES), F32)
        for cs in range(cuts):
            perm = ((slot + first == 0) & (which == cs)).astype(F32).astype(BF)
            out = out + nn(perm, sel_ref[:, cs * LANES : (cs + 1) * LANES])
        out_ref[pl.ds(pl.multiple_of(i * block, block), block), :] = out.astype(BF)


def round_kernel(in_ref, out_ref):
    out_ref.buffer[...] = in_ref.ready()[...].astype(BF)
    out_ref.send()


def serve_kernel(ent_ref, idx_ref, out_ref, sel_ref):
    fill_container(out_ref, sel_ref, ent_ref, idx_ref, 0)


def tail_kernel(rnd, ent_ref, rel_ref, par_ref, head_ref, tail_ref, kind_ref, tq_ref, at_ref, n_ref, dtail_ref, pick_ref):
    rows = ent_ref.shape[0]
    kinds = rel_ref.buffer.shape[0]
    now = slice(rnd, rnd + 1)
    pick_ref[...] = one_hot_rows(kinds * rows, kind_ref[now] * rows + head_ref[now])
    tail = tail_ref[now]
    ones = jnp.ones((8, tail.shape[1]), F32).astype(BF)
    n = nt(ones, pick_ref[...])
    n_ref[...] = n
    rel = rel_ref.ready()

    @pl.loop(0, kinds)
    def _(t):
        cut = pl.ds(pl.multiple_of(t * rows, rows), rows)
        tq_ref[cut, :] = nn(ent_ref[...], rel[t]).astype(BF)

    block = rows // 2

    @pl.loop(0, 2)
    def _(i):
        cut = pl.ds(pl.multiple_of(i * block, block), block)
        pick_t = iota((block, tail.shape[1]), 0) + i * block == tail
        c = jnp.sum(pick_t.astype(F32), axis=1, keepdims=True)
        joint = nt(pick_t.astype(F32).astype(BF), pick_ref[...])
        prob = jax.nn.sigmoid(nt(par_ref[cut, :], tq_ref[...]))
        weight = (negative_weight * c) * n[:1]
        at = (weight * prob + joint * ((1.0 - negative_weight) * prob - 1.0)).astype(BF)
        at_ref[cut, :] = at
        dtail_ref[cut, :] = nn(at, tq_ref[...]).astype(BF)


def neg_kernel(con_ref, tq_ref, n_ref, neg_ref, an_ref, dneg_ref):
    slots, width = neg_ref.shape
    cuts = width // LANES
    slot = iota((slots, con_ref.shape[0]), 0)
    row = iota((slots, con_ref.shape[0]), 1) - ((slot // NCAP) * (NCAP * cuts) + slot % NCAP)

    @pl.loop(0, cuts)
    def _(cs):
        perm = (row == cs * NCAP).astype(F32).astype(BF)
        cut = pl.ds(pl.multiple_of(cs * LANES, LANES), LANES)
        neg_ref[:, cut] = nn(perm, con_ref[...]).astype(BF)

    wide = dneg_ref.shape[1]
    prob = jax.nn.sigmoid(nt(neg_ref[...], tq_ref[...]))
    an_ref[...] = (negative_weight * n_ref[:1] * prob).astype(BF)
    dneg = nn(an_ref[...], tq_ref[...]).astype(BF)
    for cs in range(width // wide):
        dneg_ref[cs * slots : (cs + 1) * slots, :] = dneg[:, cs * wide : (cs + 1) * wide]


def head_kernel(at_ref, an_ref, par_ref, neg_ref, rel_ref, tail_ref, *refs):
    sum_ref, cut_ref = refs[-2:]
    g_ref = refs[-3]
    reps, rows, wide = cut_ref.shape
    out_refs = refs[-3 - reps : -3]
    idx_refs = refs[: -3 - reps]
    kinds = rel_ref.buffer.shape[0]
    sum_ref[...] = tail_ref[...].astype(F32)
    rel = None
    for t in range(kinds):
        cut = slice(t * rows, (t + 1) * rows)
        g = (tn(at_ref[:, cut], par_ref[...]) + tn(an_ref[:, cut], neg_ref[...])).astype(BF)
        g_ref.buffer[cut, :] = g
        rel = rel_ref.ready() if rel is None else rel
        sum_ref[...] += nt(g, rel[t])
    g_ref.send()
    for cs in range(reps):
        cut_ref[cs] = sum_ref[:, cs * wide : (cs + 1) * wide].astype(BF)
    mine = lax.axis_index("rep")
    for s in range(reps):
        out_refs[s][:rows, :] = cut_ref[lax.rem(mine + s, reps)]
        for idx_ref in idx_refs:
            out_refs[s][rows:, :] = idx_ref[...]


def rel_kernel(*refs):
    given_ref, kept_ref, ents_ref = refs[2 * ROUNDS :]
    rows, width = ents_ref.shape[1:]
    for r in range(ROUNDS):
        ents_ref[r] = refs[r].ready()[...].astype(BF)
    g_refs = [ref.ready() for ref in refs[ROUNDS : 2 * ROUNDS]]
    core = lax.rem(lax.axis_index("dom"), 2)
    block = width // 4

    def half(which, out_ref):
        cut = pl.ds(pl.multiple_of(which * rows, rows), rows)

        @pl.loop(0, 4)
        def _(i):
            part = pl.ds(pl.multiple_of(i * block, block), block)
            total = sum(tn(ents_ref[r, :, part], g_refs[r][cut, :]) for r in range(ROUNDS))
            out_ref[part, :] = total.astype(out_ref.dtype)

    half(core, kept_ref.buffer)
    kept_ref.send()
    half(1 - core, given_ref)


def pair_kernel(kept_ref, got_ref, out_ref):
    out_ref[...] = (kept_ref.ready()[...] + got_ref[...].astype(F32)).astype(BF)


def join_kernel(rnd, neg_ref, *refs):
    reps = (len(refs) - 1) // 2
    part_refs, idx_refs, out_refs = refs[:reps], refs[reps : 2 * reps], refs[2 * reps :]
    out_ref = out_refs[0]
    rows = out_ref.shape[1]
    slots = neg_ref.shape[0] // reps
    lines = slots // LANES
    mine = lax.axis_index("rep")
    total = part_refs[0][:rows, :].astype(F32)
    for part_ref in part_refs[1:]:
        total = total + part_ref[:rows, :].astype(F32)
    for s, idx_ref in enumerate(idx_refs):
        first = idx_ref.shape[0] - INDEX_LINES + rnd * lines
        for line in range(lines):
            start = lax.rem(mine + reps - s, reps) * slots + line * LANES
            index = idx_ref[first + line : first + line + 1, :].astype(F32).astype(jnp.int32)
            total = total + nn(one_hot_rows(rows, index), neg_ref[pl.ds(pl.multiple_of(start, LANES), LANES), :])
    out_ref[...] = jnp.broadcast_to(total.astype(BF)[None], out_ref.shape)


def update(grad_ref, ent_ref, acc_ref, new_ref):
    reps, _, wide = grad_ref.shape
    grads = [grad_ref[j].astype(F32) for j in range(reps)]
    square = sum(jnp.sum(g * g, axis=-1, keepdims=True) for g in grads)
    acc = acc_ref[...] + square / (reps * wide)
    scale = entity_rate / jnp.sqrt(acc)
    ent = ent_ref.ready()
    for j in range(reps):
        cut = slice(j * wide, (j + 1) * wide)
        new_ref[:, cut] = ent[:, cut] - scale * grads[j]
    return acc


def last_update_kernel(*refs):
    ent_ref, acc_ref, new_ref, new_acc_ref, grad_ref = refs[-5:]
    reps = grad_ref.shape[0]
    mine = lax.axis_index("rep")
    for s, part_ref in enumerate(refs[:-5]):
        grad_ref[lax.rem(mine + s, reps)] = part_ref[...]
    acc = update(grad_ref, ent_ref, acc_ref, new_ref)
    new_acc_ref[...] = jnp.broadcast_to(acc, (acc.shape[0], LANES)).T[:8]


def update_kernel(rnd, grad_ref, ent_ref, acc_ref, idx_ref, new_acc_ref, bf_ref, con_ref, new_ref, keep_ref, sel_ref):
    new_acc_ref[...] = update(grad_ref, ent_ref, acc_ref, new_ref.buffer)
    new_ref.send()
    bf_ref[...] = new_ref.buffer[...].astype(BF)
    keep_ref.buffer[...] = bf_ref[...]
    keep_ref.send()
    fill_container(con_ref, sel_ref, bf_ref, idx_ref, rnd + 1)


def total_kernel(parts_ref, out_ref):
    parts, piece, width = parts_ref.shape
    pairs = parts_ref[...].reshape(parts // 2, 2, piece, width)
    total = jnp.sum(pairs.astype(F32), axis=0).astype(BF).reshape(2 * piece, width)
    out_ref[...] = jnp.broadcast_to(total[None], out_ref.shape)


def step(entities, ent_accum, relations, rel_accum, heads, tails, relation_ids, negatives):
    rows, width = entities.shape
    parts = lax.axis_size("dom")
    reps = lax.axis_size("rep")
    kinds = relations.shape[0]
    slots = parts * NCAP
    wide = width // reps
    cuts = width // LANES
    everyone = ("rep", "dom")

    asked = negatives.reshape(ROUNDS, parts, NCAP).transpose(1, 0, 2).reshape(parts, ROUNDS * NCAP)
    asked = all_ways(asked, "dom").reshape(parts, ROUNDS, NCAP).transpose(1, 0, 2)
    own = asked.reshape(ROUNDS, slots)
    asked = asked.reshape(ROUNDS * slots // LANES, LANES)
    asked = jnp.pad(asked, ((0, INDEX_LINES - asked.shape[0]), (0, 0))).astype(BF)

    ent_bf = entities.astype(BF)
    accum = ent_accum.reshape(rows, 1)
    chosen = pltpu.VMEM((slots, width), BF)
    (con,) = call(serve_kernel, [((parts * cuts * NCAP, LANES), BF)], ent_bf, own, scratch=[chosen])
    ents, gs = [entities], []
    (rel_bf,) = call(round_kernel, [(relations.shape, BF)], relations, late={0: kinds}, far=(0,))
    for rnd in range(ROUNDS):
        offset = rnd + 1
        last = rnd == ROUNDS - 1
        partner = from_behind(ent_bf, "dom", -offset)
        con = all_ways(con.reshape(parts, cuts * NCAP, LANES), "dom").reshape(parts * cuts * NCAP, LANES)
        tq, at, n, dtail = call(
            functools.partial(tail_kernel, rnd),
            [((kinds * rows, width), BF), ((rows, kinds * rows), BF), ((8, kinds * rows), F32), ((rows, width), BF)],
            ent_bf,
            rel_bf,
            partner,
            heads,
            tails,
            relation_ids,
            late={1: kinds},
            scratch=[pltpu.VMEM((kinds * rows, heads.shape[1]), BF)],
        )
        dtail = from_behind(dtail, "dom", offset)
        lines = 0 if rnd else INDEX_LINES
        neg, an, dneg = call(
            neg_kernel,
            [((slots, width), BF), ((slots, kinds * rows), BF), ((reps * slots, wide), BF)],
            con,
            tq,
            n,
        )
        dneg = all_ways(dneg.reshape(reps * parts, NCAP, wide), everyone).reshape(reps * slots, wide)
        *dhead, g = call(
            head_kernel,
            [((rows + lines, wide), BF)] * reps + [((kinds * rows, width), BF)],
            at,
            an,
            partner,
            neg,
            rel_bf,
            dtail,
            *([] if rnd else [asked]),
            late={4: kinds},
            far=(reps,),
            scratch=[pltpu.VMEM((rows, width), F32), pltpu.VMEM((reps, rows, wide), BF)],
        )
        gs.append(g)
        for s in range(1, reps):
            dhead[s] = from_behind(dhead[s], "rep", s)
        if rnd == 0:
            served = dhead
        (grads,) = call(
            functools.partial(join_kernel, rnd), [((1 if last else reps, rows, wide), BF)], dneg, *dhead, *served
        )
        if rnd == 0:
            served = [part[rows:] for part in dhead]
        if last:
            parts_of = [grads[0]]
            for s in range(1, reps):
                parts_of.append(from_behind(grads[0], "rep", -s))
        else:
            grads = all_ways(grads, "rep")
        if last:
            entities, accum = call(
                last_update_kernel,
                [((rows, width), F32), ((8, rows), F32)],
                *parts_of,
                entities,
                accum,
                late={reps: rows},
                scratch=[pltpu.VMEM((reps, rows, wide), BF)],
            )
        else:
            accum, ent_bf, con, entities, keep = call(
                functools.partial(update_kernel, rnd),
                [
                    ((rows, 1), F32),
                    ((rows, width), BF),
                    ((parts * cuts * NCAP, LANES), BF),
                    ((rows, width), F32),
                    ((rows, width), BF),
                ],
                grads,
                entities,
                accum,
                own,
                late={1: rows},
                far=(3, 4),
                scratch=[chosen],
            )
            ents.append(keep)
    pair = [(i ^ 1, i) for i in range(parts)]
    given, kept = call(
        rel_kernel,
        [((width, width), BF), ((width, width), F32)],
        *ents,
        *gs,
        late={i: rows if i < ROUNDS else kinds * rows for i in range(2 * ROUNDS)},
        far=(1,),
        scratch=[pltpu.VMEM((ROUNDS, rows, width), BF)],
    )
    got = lax.ppermute(given, "dom", pair)
    (drel,) = call(pair_kernel, [((width, width), BF)], kept, got, late={0: width})
    piece = width // parts
    drel = all_ways(drel.reshape(parts, piece, width), "dom")
    (total,) = call(total_kernel, [((parts, kinds * piece, width), BF)], drel)
    total = all_ways(total, "dom")
    total = total.reshape(parts, kinds, piece, width).transpose(1, 0, 2, 3).reshape(kinds, width, width)
    total = total.astype(F32)
    new_rel_accum = rel_accum + total * total
    new_relations = relations - relation_rate * total * lax.rsqrt(new_rel_accum)
    return (entities, accum[0], new_relations, new_rel_accum)


def solution(mesh):
    in_specs = (
        P("dom", None),
        P("dom"),
        P("rep", None, None),
        P("rep", None, None),
        P(None, ("dom", "rep")),
        P(None, ("dom", "rep")),
        P(None, ("dom", "rep")),
        P(None, ("dom", "rep")),
    )
    out_specs = (P("dom", None), P("dom"), P("rep", None, None), P("rep", None, None))
    return jax.shard_map(step, mesh=mesh, in_specs=in_specs, out_specs=out_specs, check_vma=False)
```

```python
import functools
import math

import jax
import jax.numpy as jnp
from jax import lax
from jax.experimental import pallas as pl
from jax.experimental.pallas import tpu as pltpu
from jax.sharding import PartitionSpec as P


NCAP = 4
ROUNDS = 3
LANES = 128
INDEX_LINES = 16
FAR = 4 << 20

negative_weight = 0.0625
entity_rate = 0.05
relation_rate = 0.02

BF = jnp.bfloat16
F32 = jnp.float32


class Late:
    def __init__(self, source, target, buffer, sem):
        self.copy = pltpu.make_async_copy(source, target, sem)
        self.buffer = buffer

    def ready(self):
        self.copy.wait()
        return self.buffer

    def send(self):
        self.copy.start()


def call(kernel, outs, *args, late=None, far=(), scratch=(), vmem=53500):
    late = late or {}
    shapes = []
    for i, (shape, dtype) in enumerate(outs):
        whole = shape
        if i in far:
            row = math.prod(shape[1:]) * jnp.dtype(dtype).itemsize
            whole = (max(shape[0], FAR // row),) + tuple(shape[1:])
        shapes.append(jax.ShapeDtypeStruct(whole, dtype))
    moved = sum(math.prod(shape) * jnp.dtype(dtype).itemsize for shape, dtype in outs)
    moved += sum((a.size if i not in late else a.size // a.shape[0] * late[i]) * a.dtype.itemsize for i, a in enumerate(args))
    near = pl.BlockSpec(memory_space=pltpu.VMEM)
    hbm = pl.BlockSpec(memory_space=pltpu.HBM)
    count = len(late) + len(far)
    buffers = [pltpu.VMEM((late[i],) + args[i].shape[1:], args[i].dtype) for i in late]
    buffers += [pltpu.VMEM(*outs[i]) for i in far]
    sems = [pltpu.SemaphoreType.DMA((count,))] if count else []

    def body(*refs):
        refs = list(refs)
        sem = refs.pop() if count else None
        bufs = refs[len(refs) - count :]
        refs = refs[: len(refs) - count]
        for b, i in enumerate(late):
            refs[i] = Late(refs[i].at[: late[i]], bufs[b], bufs[b], sem.at[b])
            refs[i].send()
        sent = []
        for b, i in enumerate(far, len(late)):
            out = refs[len(args) + i].at[: outs[i][0][0]]
            refs[len(args) + i] = Late(bufs[b], out, bufs[b], sem.at[b])
            sent.append(refs[len(args) + i])
        kernel(*refs)
        for item in sent:
            item.ready()

    return pl.pallas_call(
        body,
        out_shape=shapes,
        in_specs=[hbm if i in late else near for i in range(len(args))],
        out_specs=[hbm if i in far else near for i in range(len(outs))],
        scratch_shapes=list(scratch) + buffers + sems,
        compiler_params=pltpu.CompilerParams(vmem_limit_bytes=vmem << 10),
        cost_estimate=pl.CostEstimate(flops=0, bytes_accessed=moved, transcendentals=0),
    )(*args)


def nn(a, b):
    return jnp.dot(a, b, preferred_element_type=F32)


def nt(a, b):
    return lax.dot_general(a, b, (((1,), (1,)), ((), ())), preferred_element_type=F32)


def tn(a, b):
    return lax.dot_general(a, b, (((0,), (0,)), ((), ())), preferred_element_type=F32)


def iota(shape, dim):
    return lax.broadcasted_iota(jnp.int32, shape, dim)


def one_hot_rows(count, index):
    return (iota((count, index.shape[1]), 0) == index).astype(F32).astype(BF)


def all_ways(block, axes):
    return lax.all_to_all(block, axes, split_axis=0, concat_axis=0, tiled=True)


def from_behind(block, axis, distance):
    n = lax.axis_size(axis)
    return lax.ppermute(block, axis, [((i - distance) % n, i) for i in range(n)])


def container_cells(parts, cuts):
    for cs in range(cuts):
        for k in range(NCAP):
            yield cs, pl.ds(k, parts, stride=NCAP), pl.ds(cs * NCAP + k, parts, stride=NCAP * cuts)


def fill_container(out_ref, sel_ref, buf_ref, ent_ref, idx_ref, rnd):
    cuts, slots, lanes = sel_ref.shape
    picked = tn(one_hot_rows(ent_ref.shape[0], idx_ref[rnd : rnd + 1]), ent_ref[...])
    for cs in range(cuts):
        sel_ref[cs] = picked[:, cs * lanes : (cs + 1) * lanes]
    for cs, rows, cells in container_cells(slots // NCAP, cuts):
        buf_ref[cells, :] = sel_ref[cs, rows, :]
    out_ref[...] = buf_ref[...].astype(BF)


def round_kernel(in_ref, out_ref):
    out_ref.buffer[...] = in_ref.ready()[...].astype(BF)
    out_ref.send()


def serve_kernel(ent_ref, idx_ref, out_ref, sel_ref, buf_ref):
    fill_container(out_ref, sel_ref, buf_ref, ent_ref, idx_ref, 0)


def tail_kernel(rnd, ent_ref, rel_ref, par_ref, head_ref, tail_ref, kind_ref, tq_ref, at_ref, n_ref, dtail_ref, pick_ref):
    rows = ent_ref.shape[0]
    kinds = rel_ref.buffer.shape[0]
    now = slice(rnd, rnd + 1)
    pick_ref[...] = one_hot_rows(kinds * rows, kind_ref[now] * rows + head_ref[now])
    tail = tail_ref[now]
    ones = jnp.ones((8, tail.shape[1]), F32).astype(BF)
    n = nt(ones, pick_ref[...])
    n_ref[...] = n
    rel = rel_ref.ready()

    @pl.loop(0, kinds)
    def _(t):
        cut = pl.ds(pl.multiple_of(t * rows, rows), rows)
        tq_ref[cut, :] = nn(ent_ref[...], rel[t]).astype(BF)

    block = rows // 2

    @pl.loop(0, 2)
    def _(i):
        cut = pl.ds(pl.multiple_of(i * block, block), block)
        pick_t = iota((block, tail.shape[1]), 0) + i * block == tail
        c = jnp.sum(pick_t.astype(F32), axis=1, keepdims=True)
        joint = nt(pick_t.astype(F32).astype(BF), pick_ref[...])
        prob = jax.nn.sigmoid(nt(par_ref[cut, :], tq_ref[...]))
        weight = (negative_weight * c) * n[:1]
        at = (weight * prob + joint * ((1.0 - negative_weight) * prob - 1.0)).astype(BF)
        at_ref[cut, :] = at
        dtail_ref[cut, :] = nn(at, tq_ref[...]).astype(BF)


def neg_kernel(con_ref, tq_ref, n_ref, neg_ref, an_ref, dneg_ref, sel_ref, buf_ref):
    slots, width = neg_ref.shape
    buf_ref[...] = con_ref[...].astype(F32)
    for cs, rows, cells in container_cells(slots // NCAP, width // LANES):
        sel_ref[cs, rows, :] = buf_ref[cells, :]
    for cs in range(width // LANES):
        neg_ref[:, cs * LANES : (cs + 1) * LANES] = sel_ref[cs].astype(BF)
    wide = dneg_ref.shape[1]
    prob = jax.nn.sigmoid(nt(neg_ref[...], tq_ref[...]))
    an_ref[...] = (negative_weight * n_ref[:1] * prob).astype(BF)
    dneg = nn(an_ref[...], tq_ref[...]).astype(BF)
    for cs in range(width // wide):
        dneg_ref[cs * slots : (cs + 1) * slots, :] = dneg[:, cs * wide : (cs + 1) * wide]


def head_kernel(at_ref, an_ref, par_ref, neg_ref, rel_ref, tail_ref, *refs):
    sum_ref, cut_ref = refs[-2:]
    g_ref = refs[-3]
    reps, rows, wide = cut_ref.shape
    out_refs = refs[-3 - reps : -3]
    idx_refs = refs[: -3 - reps]
    kinds = rel_ref.buffer.shape[0]
    sum_ref[...] = tail_ref[...].astype(F32)
    rel = None
    for t in range(kinds):
        cut = slice(t * rows, (t + 1) * rows)
        g = (tn(at_ref[:, cut], par_ref[...]) + tn(an_ref[:, cut], neg_ref[...])).astype(BF)
        g_ref.buffer[cut, :] = g
        rel = rel_ref.ready() if rel is None else rel
        sum_ref[...] += nt(g, rel[t])
    g_ref.send()
    for cs in range(reps):
        cut_ref[cs] = sum_ref[:, cs * wide : (cs + 1) * wide].astype(BF)
    mine = lax.axis_index("rep")
    for s in range(reps):
        out_refs[s][:rows, :] = cut_ref[lax.rem(mine + s, reps)]
        for idx_ref in idx_refs:
            out_refs[s][rows:, :] = idx_ref[...]


def early_kernel(*refs):
    out_ref = refs[-1]
    count = len(refs) // 2
    rows = refs[0].buffer.shape[0]
    ents = [ref.ready()[...].astype(BF) for ref in refs[:count]]
    gs = [ref.ready() for ref in refs[count:-1]]
    kinds = gs[0].shape[0] // rows
    pieces, _, line, width = out_ref.buffer.shape
    for t in range(kinds):
        total = sum(tn(ent, g[t * rows : (t + 1) * rows, :]) for ent, g in zip(ents, gs))
        part = pieces // kinds
        out_ref.buffer[t * part : (t + 1) * part] = total.reshape(part, 2, line, width)
    out_ref.send()


def rel_kernel(ent_ref, g_ref, early_ref, given_ref, kept_ref, full_ref):
    rows = ent_ref.buffer.shape[0]
    ent, g = ent_ref.ready(), g_ref.ready()
    pieces, _, line, width = full_ref.shape
    kinds = g.shape[0] // rows
    part = pieces // kinds
    early = None
    for t in range(kinds):
        total = tn(ent[...], g[t * rows : (t + 1) * rows, :]).reshape(part, 2, line, width)
        early = early_ref.ready() if early is None else early
        full_ref[t * part : (t + 1) * part] = total + early[t * part : (t + 1) * part]
    core = lax.rem(lax.axis_index("dom"), 2)
    given_ref[...] = full_ref[:, 1 - core].reshape(given_ref.shape).astype(BF)
    kept_ref.buffer[...] = full_ref[:, core].reshape(given_ref.shape)
    kept_ref.send()


def pair_kernel(kept_ref, got_ref, out_ref):
    out_ref[...] = (kept_ref.ready()[...] + got_ref[...].astype(F32)).astype(BF)


def join_kernel(rnd, neg_ref, *refs):
    reps = (len(refs) - 1) // 2
    part_refs, idx_refs, out_refs = refs[:reps], refs[reps : 2 * reps], refs[2 * reps :]
    out_ref = out_refs[0]
    rows = out_ref.shape[1]
    slots = neg_ref.shape[0] // reps
    lines = slots // LANES
    mine = lax.axis_index("rep")
    total = part_refs[0][:rows, :].astype(F32)
    for part_ref in part_refs[1:]:
        total = total + part_ref[:rows, :].astype(F32)
    for s, idx_ref in enumerate(idx_refs):
        first = idx_ref.shape[0] - INDEX_LINES + rnd * lines
        for line in range(lines):
            start = lax.rem(mine + reps - s, reps) * slots + line * LANES
            index = idx_ref[first + line : first + line + 1, :].astype(F32).astype(jnp.int32)
            total = total + nn(one_hot_rows(rows, index), neg_ref[pl.ds(pl.multiple_of(start, LANES), LANES), :])
    out_ref[...] = jnp.broadcast_to(total.astype(BF)[None], out_ref.shape)


def update(grad_ref, ent_ref, acc_ref, new_ref):
    reps, _, wide = grad_ref.shape
    grads = [grad_ref[j].astype(F32) for j in range(reps)]
    square = sum(jnp.sum(g * g, axis=-1, keepdims=True) for g in grads)
    acc = acc_ref[...] + square / (reps * wide)
    scale = entity_rate / jnp.sqrt(acc)
    ent = ent_ref.ready()
    for j in range(reps):
        cut = slice(j * wide, (j + 1) * wide)
        new_ref[:, cut] = ent[:, cut] - scale * grads[j]
    return acc


def last_update_kernel(*refs):
    ent_ref, acc_ref, new_ref, new_acc_ref, grad_ref = refs[-5:]
    reps = grad_ref.shape[0]
    mine = lax.axis_index("rep")
    for s, part_ref in enumerate(refs[:-5]):
        grad_ref[lax.rem(mine + s, reps)] = part_ref[...]
    acc = update(grad_ref, ent_ref, acc_ref, new_ref)
    new_acc_ref[...] = jnp.broadcast_to(acc, (acc.shape[0], LANES)).T[:8]


def update_kernel(rnd, grad_ref, ent_ref, acc_ref, idx_ref, new_acc_ref, bf_ref, con_ref, new_ref, keep_ref, sel_ref, buf_ref):
    new_acc_ref[...] = update(grad_ref, ent_ref, acc_ref, new_ref.buffer)
    new_ref.send()
    bf_ref[...] = new_ref.buffer[...].astype(BF)
    keep_ref.buffer[...] = bf_ref[...]
    keep_ref.send()
    fill_container(con_ref, sel_ref, buf_ref, bf_ref, idx_ref, rnd + 1)


def total_kernel(parts_ref, out_ref):
    parts, piece, width = parts_ref.shape
    pairs = parts_ref[...].reshape(parts // 2, 2, piece, width)
    total = jnp.sum(pairs.astype(F32), axis=0).astype(BF).reshape(2 * piece, width)
    out_ref[...] = jnp.broadcast_to(total[None], out_ref.shape)


def step(entities, ent_accum, relations, rel_accum, heads, tails, relation_ids, negatives):
    rows, width = entities.shape
    parts = lax.axis_size("dom")
    reps = lax.axis_size("rep")
    kinds = relations.shape[0]
    slots = parts * NCAP
    wide = width // reps
    cuts = width // LANES
    everyone = ("rep", "dom")

    asked = negatives.reshape(ROUNDS, parts, NCAP).transpose(1, 0, 2).reshape(parts, ROUNDS * NCAP)
    asked = all_ways(asked, "dom").reshape(parts, ROUNDS, NCAP).transpose(1, 0, 2)
    own = asked.reshape(ROUNDS, slots)
    asked = asked.reshape(ROUNDS * slots // LANES, LANES)
    asked = jnp.pad(asked, ((0, INDEX_LINES - asked.shape[0]), (0, 0))).astype(BF)

    ent_bf = entities.astype(BF)
    accum = ent_accum.reshape(rows, 1)
    chosen = [pltpu.VMEM((cuts, slots, LANES), F32), pltpu.VMEM((parts * cuts * NCAP, LANES), F32)]
    (con,) = call(serve_kernel, [((parts * cuts * NCAP, LANES), BF)], ent_bf, own, scratch=chosen)
    ents, gs = [entities], []
    last_round = ROUNDS - 1
    (rel_bf,) = call(round_kernel, [(relations.shape, BF)], relations, late={0: kinds}, far=(0,))
    for rnd in range(ROUNDS):
        offset = rnd + 1
        last = rnd == ROUNDS - 1
        partner = from_behind(ent_bf, "dom", -offset)
        con = all_ways(con.reshape(parts, cuts * NCAP, LANES), "dom").reshape(parts * cuts * NCAP, LANES)
        tq, at, n, dtail = call(
            functools.partial(tail_kernel, rnd),
            [((kinds * rows, width), BF), ((rows, kinds * rows), BF), ((8, kinds * rows), F32), ((rows, width), BF)],
            ent_bf,
            rel_bf,
            partner,
            heads,
            tails,
            relation_ids,
            late={1: kinds},
            scratch=[pltpu.VMEM((kinds * rows, heads.shape[1]), BF)],
        )
        dtail = from_behind(dtail, "dom", offset)
        lines = 0 if rnd else INDEX_LINES
        if last:
            (early,) = call(
                early_kernel,
                [((parts, 2, kinds * width // (2 * parts), width), F32)],
                *ents[:-1],
                *gs,
                late={i: rows if i < last_round else kinds * rows for i in range(2 * last_round)},
                far=(0,),
            )
        neg, an, dneg = call(
            neg_kernel,
            [((slots, width), BF), ((slots, kinds * rows), BF), ((reps * slots, wide), BF)],
            con,
            tq,
            n,
            scratch=chosen,
        )
        dneg = all_ways(dneg.reshape(reps * parts, NCAP, wide), everyone).reshape(reps * slots, wide)
        *dhead, g = call(
            head_kernel,
            [((rows + lines, wide), BF)] * reps + [((kinds * rows, width), BF)],
            at,
            an,
            partner,
            neg,
            rel_bf,
            dtail,
            *([] if rnd else [asked]),
            late={4: kinds},
            far=(reps,),
            scratch=[pltpu.VMEM((rows, width), F32), pltpu.VMEM((reps, rows, wide), BF)],
        )
        gs.append(g)
        for s in range(1, reps):
            dhead[s] = from_behind(dhead[s], "rep", s)
        if rnd == 0:
            served = dhead
        (grads,) = call(
            functools.partial(join_kernel, rnd), [((1 if last else reps, rows, wide), BF)], dneg, *dhead, *served
        )
        if rnd == 0:
            served = [part[rows:] for part in dhead]
        if last:
            parts_of = [grads[0]]
            for s in range(1, reps):
                parts_of.append(from_behind(grads[0], "rep", -s))
        else:
            grads = all_ways(grads, "rep")
        if last:
            entities, accum = call(
                last_update_kernel,
                [((rows, width), F32), ((8, rows), F32)],
                *parts_of,
                entities,
                accum,
                late={reps: rows},
                scratch=[pltpu.VMEM((reps, rows, wide), BF)],
            )
        else:
            accum, ent_bf, con, entities, keep = call(
                functools.partial(update_kernel, rnd),
                [
                    ((rows, 1), F32),
                    ((rows, width), BF),
                    ((parts * cuts * NCAP, LANES), BF),
                    ((rows, width), F32),
                    ((rows, width), BF),
                ],
                grads,
                entities,
                accum,
                own,
                late={1: rows},
                far=(3, 4),
                scratch=chosen,
            )
            ents.append(keep)
    pair = [(i ^ 1, i) for i in range(parts)]
    half = kinds * width // 2
    piece = half // parts
    given, kept = call(
        rel_kernel,
        [((half, width), BF), ((half, width), F32)],
        ents[-1],
        gs[-1],
        early,
        late={0: rows, 1: kinds * rows, 2: parts},
        far=(1,),
        scratch=[pltpu.VMEM((parts, 2, piece, width), F32)],
    )
    got = lax.ppermute(given, "dom", pair)
    (drel,) = call(pair_kernel, [((half, width), BF)], kept, got, late={0: half})
    drel = all_ways(drel.reshape(parts, piece, width), "dom")
    (total,) = call(total_kernel, [((parts, 2 * piece, width), BF)], drel)
    total = all_ways(total, "dom")
    total = lax.optimization_barrier(total.reshape(kinds, width, width)).astype(F32)
    new_rel_accum = rel_accum + total * total
    new_relations = relations - relation_rate * total * lax.rsqrt(new_rel_accum)
    return (entities, accum[0], new_relations, new_rel_accum)


def solution(mesh):
    in_specs = (
        P("dom", None),
        P("dom"),
        P("rep", None, None),
        P("rep", None, None),
        P(None, ("dom", "rep")),
        P(None, ("dom", "rep")),
        P(None, ("dom", "rep")),
        P(None, ("dom", "rep")),
    )
    out_specs = (P("dom", None), P("dom"), P("rep", None, None), P("rep", None, None))
    return jax.shard_map(step, mesh=mesh, in_specs=in_specs, out_specs=out_specs, check_vma=False)
```

```python
import functools
import math

import jax
import jax.numpy as jnp
from jax import lax
from jax.experimental import pallas as pl
from jax.experimental.pallas import tpu as pltpu
from jax.sharding import PartitionSpec as P


NCAP = 4
ROUNDS = 3
LANES = 128
INDEX_LINES = 16
FAR = 4 << 20

negative_weight = 0.0625
entity_rate = 0.05
relation_rate = 0.02

BF = jnp.bfloat16
F32 = jnp.float32


class Late:
    def __init__(self, source, target, buffer, sem):
        self.copy = pltpu.make_async_copy(source, target, sem)
        self.buffer = buffer

    def ready(self):
        self.copy.wait()
        return self.buffer

    def send(self):
        self.copy.start()


def call(kernel, outs, *args, late=None, far=(), scratch=(), vmem=53500):
    late = late or {}
    shapes = []
    for i, (shape, dtype) in enumerate(outs):
        whole = shape
        if i in far:
            row = math.prod(shape[1:]) * jnp.dtype(dtype).itemsize
            whole = (max(shape[0], FAR // row),) + tuple(shape[1:])
        shapes.append(jax.ShapeDtypeStruct(whole, dtype))
    moved = sum(math.prod(shape) * jnp.dtype(dtype).itemsize for shape, dtype in outs)
    moved += sum((a.size if i not in late else a.size // a.shape[0] * late[i]) * a.dtype.itemsize for i, a in enumerate(args))
    near = pl.BlockSpec(memory_space=pltpu.VMEM)
    hbm = pl.BlockSpec(memory_space=pltpu.HBM)
    count = len(late) + len(far)
    buffers = [pltpu.VMEM((late[i],) + args[i].shape[1:], args[i].dtype) for i in late]
    buffers += [pltpu.VMEM(*outs[i]) for i in far]
    sems = [pltpu.SemaphoreType.DMA((count,))] if count else []

    def body(*refs):
        refs = list(refs)
        sem = refs.pop() if count else None
        bufs = refs[len(refs) - count :]
        refs = refs[: len(refs) - count]
        for b, i in enumerate(late):
            refs[i] = Late(refs[i].at[: late[i]], bufs[b], bufs[b], sem.at[b])
            refs[i].send()
        sent = []
        for b, i in enumerate(far, len(late)):
            out = refs[len(args) + i].at[: outs[i][0][0]]
            refs[len(args) + i] = Late(bufs[b], out, bufs[b], sem.at[b])
            sent.append(refs[len(args) + i])
        kernel(*refs)
        for item in sent:
            item.ready()

    return pl.pallas_call(
        body,
        out_shape=shapes,
        in_specs=[hbm if i in late else near for i in range(len(args))],
        out_specs=[hbm if i in far else near for i in range(len(outs))],
        scratch_shapes=list(scratch) + buffers + sems,
        compiler_params=pltpu.CompilerParams(vmem_limit_bytes=vmem << 10),
        cost_estimate=pl.CostEstimate(flops=0, bytes_accessed=moved, transcendentals=0),
    )(*args)


def nn(a, b):
    return jnp.dot(a, b, preferred_element_type=F32)


def nt(a, b):
    return lax.dot_general(a, b, (((1,), (1,)), ((), ())), preferred_element_type=F32)


def tn(a, b):
    return lax.dot_general(a, b, (((0,), (0,)), ((), ())), preferred_element_type=F32)


def iota(shape, dim):
    return lax.broadcasted_iota(jnp.int32, shape, dim)


def one_hot_rows(count, index):
    return (iota((count, index.shape[1]), 0) == index).astype(F32).astype(BF)


def all_ways(block, axes):
    return lax.all_to_all(block, axes, split_axis=0, concat_axis=0, tiled=True)


def from_behind(block, axis, distance):
    n = lax.axis_size(axis)
    return lax.ppermute(block, axis, [((i - distance) % n, i) for i in range(n)])


def container_cells(parts, cuts):
    for cs in range(cuts):
        for k in range(NCAP):
            yield cs, pl.ds(k, parts, stride=NCAP), pl.ds(cs * NCAP + k, parts, stride=NCAP * cuts)


def fill_container(out_ref, sel_ref, buf_ref, ent_ref, idx_ref, rnd):
    cuts, slots, lanes = sel_ref.shape
    picked = tn(one_hot_rows(ent_ref.shape[0], idx_ref[rnd : rnd + 1]), ent_ref[...])
    for cs in range(cuts):
        sel_ref[cs] = picked[:, cs * lanes : (cs + 1) * lanes]
    for cs, rows, cells in container_cells(slots // NCAP, cuts):
        buf_ref[cells, :] = sel_ref[cs, rows, :]
    out_ref[...] = buf_ref[...].astype(BF)


def round_kernel(in_ref, out_ref):
    out_ref.buffer[...] = in_ref.ready()[...].astype(BF)
    out_ref.send()


def serve_kernel(ent_ref, idx_ref, out_ref, sel_ref, buf_ref):
    fill_container(out_ref, sel_ref, buf_ref, ent_ref, idx_ref, 0)


def tail_kernel(rnd, ent_ref, rel_ref, par_ref, head_ref, tail_ref, kind_ref, tq_ref, at_ref, n_ref, dtail_ref, pick_ref):
    rows = ent_ref.shape[0]
    kinds = rel_ref.buffer.shape[0]
    now = slice(rnd, rnd + 1)
    pick_ref[...] = one_hot_rows(kinds * rows, kind_ref[now] * rows + head_ref[now])
    tail = tail_ref[now]
    ones = jnp.ones((8, tail.shape[1]), F32).astype(BF)
    n = nt(ones, pick_ref[...])
    n_ref[...] = n
    rel = rel_ref.ready()

    half = rows // 2

    @pl.loop(0, 2 * kinds)
    def _(i):
        cut = pl.ds(pl.multiple_of(i * half, half), half)
        head = pl.ds(pl.multiple_of(i % 2 * half, half), half)
        tq_ref[cut, :] = nn(ent_ref[head, :], rel[i // 2]).astype(BF)

    block = rows // 4

    @pl.loop(0, 4)
    def _(i):
        cut = pl.ds(pl.multiple_of(i * block, block), block)
        pick_t = iota((block, tail.shape[1]), 0) + i * block == tail
        c = jnp.sum(pick_t.astype(F32), axis=1, keepdims=True)
        joint = nt(pick_t.astype(F32).astype(BF), pick_ref[...])
        prob = jax.nn.sigmoid(nt(par_ref[cut, :], tq_ref[...]))
        weight = (negative_weight * c) * n[:1]
        at = (weight * prob + joint * ((1.0 - negative_weight) * prob - 1.0)).astype(BF)
        at_ref[cut, :] = at
        dtail_ref[cut, :] = nn(at, tq_ref[...]).astype(BF)


def neg_kernel(con_ref, tq_ref, n_ref, neg_ref, an_ref, dneg_ref, sel_ref, buf_ref):
    slots, width = neg_ref.shape
    buf_ref[...] = con_ref[...].astype(F32)
    for cs, rows, cells in container_cells(slots // NCAP, width // LANES):
        sel_ref[cs, rows, :] = buf_ref[cells, :]
    for cs in range(width // LANES):
        neg_ref[:, cs * LANES : (cs + 1) * LANES] = sel_ref[cs].astype(BF)
    wide = dneg_ref.shape[1]
    prob = jax.nn.sigmoid(nt(neg_ref[...], tq_ref[...]))
    an_ref[...] = (negative_weight * n_ref[:1] * prob).astype(BF)
    dneg = nn(an_ref[...], tq_ref[...]).astype(BF)
    for cs in range(width // wide):
        dneg_ref[cs * slots : (cs + 1) * slots, :] = dneg[:, cs * wide : (cs + 1) * wide]


def head_kernel(at_ref, an_ref, par_ref, neg_ref, rel_ref, tail_ref, *refs):
    sum_ref, cut_ref = refs[-2:]
    g_ref = refs[-3]
    reps, rows, wide = cut_ref.shape
    out_refs = refs[-3 - reps : -3]
    idx_refs = refs[: -3 - reps]
    kinds = rel_ref.buffer.shape[0]
    sum_ref[...] = tail_ref[...].astype(F32)
    rel = None
    for t in range(kinds):
        cut = slice(t * rows, (t + 1) * rows)
        g = (tn(at_ref[:, cut], par_ref[...]) + tn(an_ref[:, cut], neg_ref[...])).astype(BF)
        g_ref.buffer[cut, :] = g
        rel = rel_ref.ready() if rel is None else rel
        sum_ref[...] += nt(g, rel[t])
    g_ref.send()
    for cs in range(reps):
        cut_ref[cs] = sum_ref[:, cs * wide : (cs + 1) * wide].astype(BF)
    mine = lax.axis_index("rep")
    for s in range(reps):
        out_refs[s][:rows, :] = cut_ref[lax.rem(mine + s, reps)]
        for idx_ref in idx_refs:
            out_refs[s][rows:, :] = idx_ref[...]


def early_kernel(*refs):
    out_ref = refs[-1]
    count = len(refs) // 2
    rows = refs[0].buffer.shape[0]
    ents = [ref.ready()[...].astype(BF) for ref in refs[:count]]
    gs = [ref.ready() for ref in refs[count:-1]]
    kinds = gs[0].shape[0] // rows
    pieces, _, line, width = out_ref.buffer.shape
    for t in range(kinds):
        total = sum(tn(ent, g[t * rows : (t + 1) * rows, :]) for ent, g in zip(ents, gs))
        part = pieces // kinds
        out_ref.buffer[t * part : (t + 1) * part] = total.reshape(part, 2, line, width)
    out_ref.send()


def rel_kernel(ent_ref, g_ref, early_ref, given_ref, kept_ref, full_ref):
    rows = ent_ref.buffer.shape[0]
    ent, g = ent_ref.ready(), g_ref.ready()
    pieces, _, line, width = full_ref.shape
    kinds = g.shape[0] // rows
    part = pieces // kinds
    early = None
    for t in range(kinds):
        total = tn(ent[...], g[t * rows : (t + 1) * rows, :]).reshape(part, 2, line, width)
        early = early_ref.ready() if early is None else early
        full_ref[t * part : (t + 1) * part] = total + early[t * part : (t + 1) * part]
    core = lax.rem(lax.axis_index("dom"), 2)
    given_ref[...] = full_ref[:, 1 - core].reshape(given_ref.shape).astype(BF)
    kept_ref.buffer[...] = full_ref[:, core].reshape(given_ref.shape)
    kept_ref.send()


def pair_kernel(kept_ref, got_ref, out_ref):
    out_ref[...] = (kept_ref.ready()[...] + got_ref[...].astype(F32)).astype(BF)


def join_kernel(rnd, neg_ref, *refs):
    reps = (len(refs) - 1) // 2
    part_refs, idx_refs, out_refs = refs[:reps], refs[reps : 2 * reps], refs[2 * reps :]
    out_ref = out_refs[0]
    rows = out_ref.shape[0]
    slots = neg_ref.shape[0] // reps
    lines = slots // LANES
    mine = lax.axis_index("rep")
    total = part_refs[0][:rows, :].astype(F32)
    for part_ref in part_refs[1:]:
        total = total + part_ref[:rows, :].astype(F32)
    for s, idx_ref in enumerate(idx_refs):
        first = idx_ref.shape[0] - INDEX_LINES + rnd * lines
        for line in range(lines):
            start = lax.rem(mine + reps - s, reps) * slots + line * LANES
            index = idx_ref[first + line : first + line + 1, :].astype(F32).astype(jnp.int32)
            total = total + nn(one_hot_rows(rows, index), neg_ref[pl.ds(pl.multiple_of(start, LANES), LANES), :])
    out_ref[...] = total.astype(BF)


def update(grad_ref, ent_ref, acc_ref, new_ref):
    reps, _, wide = grad_ref.shape
    grads = [grad_ref[j].astype(F32) for j in range(reps)]
    square = sum(jnp.sum(g * g, axis=-1, keepdims=True) for g in grads)
    acc = acc_ref[...] + square / (reps * wide)
    scale = entity_rate / jnp.sqrt(acc)
    ent = ent_ref.ready()
    for j in range(reps):
        cut = slice(j * wide, (j + 1) * wide)
        new_ref[:, cut] = ent[:, cut] - scale * grads[j]
    return acc


def place_parts(part_refs, grad_ref):
    reps = grad_ref.shape[0]
    mine = lax.axis_index("rep")
    for s, part_ref in enumerate(part_refs):
        grad_ref[lax.rem(mine + s, reps)] = part_ref[...]


def last_update_kernel(*refs):
    ent_ref, acc_ref, new_ref, new_acc_ref, grad_ref = refs[-5:]
    place_parts(refs[:-5], grad_ref)
    acc = update(grad_ref, ent_ref, acc_ref, new_ref)
    new_acc_ref[...] = jnp.broadcast_to(acc, (acc.shape[0], LANES)).T[:8]


def update_kernel(rnd, *refs):
    ent_ref, acc_ref, idx_ref, new_acc_ref, bf_ref, con_ref, new_ref, keep_ref, sel_ref, buf_ref, grad_ref = refs[-11:]
    place_parts(refs[:-11], grad_ref)
    new_acc_ref[...] = update(grad_ref, ent_ref, acc_ref, new_ref.buffer)
    new_ref.send()
    bf_ref[...] = new_ref.buffer[...].astype(BF)
    keep_ref.buffer[...] = bf_ref[...]
    keep_ref.send()
    fill_container(con_ref, sel_ref, buf_ref, bf_ref, idx_ref, rnd + 1)


def total_kernel(parts_ref, out_ref):
    parts, piece, width = parts_ref.shape
    pairs = parts_ref[...].reshape(parts // 2, 2, piece, width)
    total = jnp.sum(pairs.astype(F32), axis=0).astype(BF).reshape(2 * piece, width)
    out_ref[...] = jnp.broadcast_to(total[None], out_ref.shape)


def step(entities, ent_accum, relations, rel_accum, heads, tails, relation_ids, negatives):
    rows, width = entities.shape
    parts = lax.axis_size("dom")
    reps = lax.axis_size("rep")
    kinds = relations.shape[0]
    slots = parts * NCAP
    wide = width // reps
    cuts = width // LANES
    everyone = ("rep", "dom")

    asked = negatives.reshape(ROUNDS, parts, NCAP).transpose(1, 0, 2).reshape(parts, ROUNDS * NCAP)
    asked = all_ways(asked, "dom").reshape(parts, ROUNDS, NCAP).transpose(1, 0, 2)
    own = asked.reshape(ROUNDS, slots)
    asked = asked.reshape(ROUNDS * slots // LANES, LANES)
    asked = jnp.pad(asked, ((0, INDEX_LINES - asked.shape[0]), (0, 0))).astype(BF)

    ent_bf = entities.astype(BF)
    accum = ent_accum.reshape(rows, 1)
    placed = pltpu.VMEM((reps, rows, wide), BF)
    chosen = [pltpu.VMEM((cuts, slots, LANES), F32), pltpu.VMEM((parts * cuts * NCAP, LANES), F32)]
    (con,) = call(serve_kernel, [((parts * cuts * NCAP, LANES), BF)], ent_bf, own, scratch=chosen)
    ents, gs = [entities], []
    last_round = ROUNDS - 1
    (rel_bf,) = call(round_kernel, [(relations.shape, BF)], relations, late={0: kinds}, far=(0,))
    for rnd in range(ROUNDS):
        offset = rnd + 1
        last = rnd == ROUNDS - 1
        partner = from_behind(ent_bf, "dom", -offset)
        con = all_ways(con.reshape(parts, cuts * NCAP, LANES), "dom").reshape(parts * cuts * NCAP, LANES)
        tq, at, n, dtail = call(
            functools.partial(tail_kernel, rnd),
            [((kinds * rows, width), BF), ((rows, kinds * rows), BF), ((8, kinds * rows), F32), ((rows, width), BF)],
            ent_bf,
            rel_bf,
            partner,
            heads,
            tails,
            relation_ids,
            late={1: kinds},
            scratch=[pltpu.VMEM((kinds * rows, heads.shape[1]), BF)],
        )
        dtail = from_behind(dtail, "dom", offset)
        lines = 0 if rnd else INDEX_LINES
        if last:
            (early,) = call(
                early_kernel,
                [((parts, 2, kinds * width // (2 * parts), width), F32)],
                *ents[:-1],
                *gs,
                late={i: rows if i < last_round else kinds * rows for i in range(2 * last_round)},
                far=(0,),
            )
        neg, an, dneg = call(
            neg_kernel,
            [((slots, width), BF), ((slots, kinds * rows), BF), ((reps * slots, wide), BF)],
            con,
            tq,
            n,
            scratch=chosen,
        )
        dneg = all_ways(dneg.reshape(reps * parts, NCAP, wide), everyone).reshape(reps * slots, wide)
        *dhead, g = call(
            head_kernel,
            [((rows + lines, wide), BF)] * reps + [((kinds * rows, width), BF)],
            at,
            an,
            partner,
            neg,
            rel_bf,
            dtail,
            *([] if rnd else [asked]),
            late={4: kinds},
            far=(reps,),
            scratch=[pltpu.VMEM((rows, width), F32), pltpu.VMEM((reps, rows, wide), BF)],
        )
        gs.append(g)
        for s in range(1, reps):
            dhead[s] = from_behind(dhead[s], "rep", s)
        if rnd == 0:
            served = dhead
        (grads,) = call(
            functools.partial(join_kernel, rnd), [((rows, wide), BF)], dneg, *dhead, *served
        )
        if rnd == 0:
            served = [part[rows:] for part in dhead]
        parts_of = [grads]
        for s in range(1, reps):
            parts_of.append(from_behind(grads, "rep", -s))
        if last:
            entities, accum = call(
                last_update_kernel,
                [((rows, width), F32), ((8, rows), F32)],
                *parts_of,
                entities,
                accum,
                late={reps: rows},
                scratch=[placed],
            )
        else:
            accum, ent_bf, con, entities, keep = call(
                functools.partial(update_kernel, rnd),
                [
                    ((rows, 1), F32),
                    ((rows, width), BF),
                    ((parts * cuts * NCAP, LANES), BF),
                    ((rows, width), F32),
                    ((rows, width), BF),
                ],
                *parts_of,
                entities,
                accum,
                own,
                late={reps: rows},
                far=(3, 4),
                scratch=[*chosen, placed],
            )
            ents.append(keep)
    pair = [(i ^ 1, i) for i in range(parts)]
    half = kinds * width // 2
    piece = half // parts
    given, kept = call(
        rel_kernel,
        [((half, width), BF), ((half, width), F32)],
        ents[-1],
        gs[-1],
        early,
        late={0: rows, 1: kinds * rows, 2: parts},
        far=(1,),
        scratch=[pltpu.VMEM((parts, 2, piece, width), F32)],
    )
    got = lax.ppermute(given, "dom", pair)
    (drel,) = call(pair_kernel, [((half, width), BF)], kept, got, late={0: half})
    drel = all_ways(drel.reshape(parts, piece, width), "dom")
    (total,) = call(total_kernel, [((parts, 2 * piece, width), BF)], drel)
    total = all_ways(total, "dom")
    total = lax.optimization_barrier(total.reshape(kinds, width, width)).astype(F32)
    new_rel_accum = rel_accum + total * total
    new_relations = relations - relation_rate * total * lax.rsqrt(new_rel_accum)
    return (entities, accum[0], new_relations, new_rel_accum)


def solution(mesh):
    in_specs = (
        P("dom", None),
        P("dom"),
        P("rep", None, None),
        P("rep", None, None),
        P(None, ("dom", "rep")),
        P(None, ("dom", "rep")),
        P(None, ("dom", "rep")),
        P(None, ("dom", "rep")),
    )
    out_specs = (P("dom", None), P("dom"), P("rep", None, None), P("rep", None, None))
    return jax.shard_map(step, mesh=mesh, in_specs=in_specs, out_specs=out_specs, check_vma=False)
```
